32 devices in a mesh: prow: 8 (over z, y), pcol: 4 (over x, core).
Axes of the slice: x: 2, y: 2, z: 4, core: 2. Of those that a mesh axis runs over, the one named last changes fastest.
Arguments:
- b_panel: float32 [1024, 512], P('prow'), may hold values from -6 to 6
- b_rest: float32 [8192, 512], P('prow'), may hold values from -6 to 6
- u_diag: float32 [1024, 1024], P('prow', 'pcol'), as said below
- u_panel: float32 [1024, 8192], P('pcol', 'prow'), may hold values from -0.1875 to 0.1875
- l_diag: float32 [1024, 1024], P('prow', 'pcol'), as said below
- l_below: float32 [8192, 1024], P('prow', 'pcol'), may hold values from -0.09375 to 0.09375
- v_below: float32 [8192, 512], P('prow'), may hold values from -6 to 6
- pivot: int32 [1024], replicated, may hold values from 0 to 8191, as said below
Outputs:
- w_rest: float32 [8192, 512], P('prow')
- x_panel: float32 [1024, 512], P('prow')
- x_rest: float32 [8192, 512], P('prow')
The draws below stay inside these ranges and needn't reach their ends.
Inputs may be any that keep to these rules, and one draw needn't show every extreme that they name: `pivot`: the 1024 entries are distinct, so the interchanges are disjoint. `u_diag`: upper triangular; its diagonal lies in 1 to 2. `l_diag`: lower triangular; its diagonal is one.
All inputs are finite; a program needn't handle non-finite values.
Results may differ from the reference program's by a relative error of at most 0.00007.
Values sent between devices are 32-bit elements; how exact they have to be, the bound alone decides.
A program may use at most 128 MiB of HBM per device.

```python
import jax
import jax.numpy as jnp
from jax import lax

NB = 1024
RHS = 512
ROWS_DEV = 1024
ROWS = 8192
N_PROW = 8


def draw_u_diag(key, part):
    first_key, second_key = jax.random.split(key)
    spread = 0.5 * jax.random.normal(first_key, (NB, NB), jnp.float32) / jnp.sqrt(jnp.float32(NB))
    diag_vals = jax.random.uniform(second_key, (NB,), jnp.float32, 1.0, 2.0)
    row_index = jnp.arange(NB)[:, None]
    col_index = jnp.arange(NB)[None, :]
    upper = jnp.where(col_index > row_index, spread, 0.0)
    return upper + jnp.where(col_index == row_index, diag_vals[:, None], 0.0)


def draw_l_diag(key, part):
    spread = 0.5 * jax.random.normal(key, (NB, NB), jnp.float32) / jnp.sqrt(jnp.float32(NB))
    row_index = jnp.arange(NB)[:, None]
    col_index = jnp.arange(NB)[None, :]
    lower = jnp.where(col_index < row_index, spread, 0.0)
    return lower + jnp.where(col_index == row_index, 1.0, 0.0)


def draw_pivot(key, part):
    group = NB // N_PROW
    clustered = N_PROW // 4
    key_src, key_dst, key_off, key_rest = jax.random.split(key, 4)
    sources = (jax.random.permutation(key_src, N_PROW - 2) + 1).astype(jnp.int32)[:clustered]
    targets = jax.random.permutation(key_dst, N_PROW).astype(jnp.int32)[:clustered]
    offsets = jax.random.randint(key_off, (clustered,), 0, ROWS_DEV - group + 1).astype(jnp.int32)
    shuffled = (jax.random.permutation(key_rest, ROWS - 2) + 1).astype(jnp.int32)
    row_source = shuffled // ROWS_DEV
    taken = jnp.any(row_source[:, None] == sources[None, :], axis=1).astype(jnp.int32)
    order = jnp.argsort(taken, stable=True)
    head = jnp.array([ROWS - 1, 0], jnp.int32)
    pool = jnp.concatenate([head, shuffled[order]]).astype(jnp.int32)
    panel_index = jnp.arange(NB, dtype=jnp.int32)
    target_of = panel_index // group
    match = target_of[:, None] == targets[None, :]
    is_clustered = jnp.any(match, axis=1)
    run_start = jnp.sum(jnp.where(match, sources[None, :] * ROWS_DEV + offsets[None, :], 0), axis=1).astype(jnp.int32)
    cluster_row = run_start + panel_index % group
    free_rank = (jnp.cumsum(1 - is_clustered.astype(jnp.int32)) - 1).astype(jnp.int32)
    free_row = pool[jnp.clip(free_rank, 0, NB - 1).astype(jnp.int32)]
    return jnp.where(is_clustered, cluster_row, free_row).astype(jnp.int32)


def spiked(drawn, rng, source, target, parts, factor):
    owner, partner = [(jnp.arange(drawn.shape[dim]) // (drawn.shape[dim] // parts)).reshape([-1 if axis == dim else 1 for axis in range(drawn.ndim)]) for dim in (source, target)]
    chosen = jax.random.permutation(rng, parts)[partner]
    strong = (owner == chosen) | (owner == (partner + parts // 2) % parts)
    return jnp.where(strong, factor * drawn, drawn)


def block_levels(stream_key, shape, cuts, low, top_value):
    gain = 1.0
    for dim, shards_of in cuts:
        heights = jax.random.uniform(jax.random.fold_in(jax.random.fold_in(stream_key, 6), dim), (shards_of,), jnp.float32, low / len(cuts), top_value / len(cuts))
        gain = gain * jnp.repeat(jnp.exp(heights), shape[dim] // shards_of).reshape((-1,) + (1,) * (len(shape) - 1 - dim))
    return gain


def gaussian(rng, shape, scale, bound, shards=(), held_as=jnp.bfloat16):
    entries = scale * jax.random.normal(rng, shape, jnp.float32)
    if shards:
        entries = entries * block_levels(rng, shape, shards, -0.22, 0.18)
    return jnp.clip(entries, -bound, bound).astype(held_as)


def heavy_noise(own_key, dims, width, limit, shards, heavy, kind=jnp.bfloat16):
    drawn = width * jax.random.normal(own_key, dims, jnp.float32)
    if shards:
        drawn = drawn * block_levels(own_key, dims, shards, -0.22, 0.18)
    return jnp.clip(spiked(drawn, jax.random.fold_in(own_key, 3), *heavy), -limit, limit).astype(kind)


def setup_inputs(seed: int = 0) -> dict:
    keys = jax.random.split(jax.random.key(seed), 9)
    b_panel = gaussian(keys[0], (NB, RHS), 1.0, 6.0, ((0, 8),), jnp.float32)
    b_rest = gaussian(keys[1], (ROWS, RHS), 1.0, 6.0, ((0, 8),), jnp.float32)
    u_diag = draw_u_diag(jax.random.fold_in(keys[8], 71), 0)
    u_panel = gaussian(keys[3], (NB, ROWS), NB ** -0.5, 0.1875, ((0, 4), (1, 8)), jnp.float32)
    l_diag = draw_l_diag(jax.random.fold_in(keys[8], 71), 0)
    l_below = heavy_noise(keys[5], (ROWS, NB), ROWS ** -0.5, 0.09375, ((0, 8), (1, 4)), (0, 1, 8, 2.0), jnp.float32)
    v_below = gaussian(keys[6], (ROWS, RHS), 1.0, 6.0, ((0, 8),), jnp.float32)
    pivot = draw_pivot(jax.random.fold_in(keys[8], 71), 0)
    return dict(b_panel=b_panel, b_rest=b_rest, u_diag=u_diag, u_panel=u_panel, l_diag=l_diag, l_below=l_below, v_below=v_below, pivot=pivot)


def reference(b_panel, b_rest, u_diag, u_panel, l_diag, l_below, v_below, pivot):
    highest = lax.Precision.HIGHEST
    w_panel = lax.linalg.triangular_solve(u_diag, b_panel, left_side=True, lower=False, transpose_a=True)
    update = lax.dot_general(u_panel.astype(jnp.float32), w_panel.astype(jnp.float32), (((0,), (0,)), ((), ())), precision=highest, preferred_element_type=jnp.float32)
    w_rest = b_rest - update
    coupling = lax.dot_general(l_below.astype(jnp.float32), v_below.astype(jnp.float32), (((0,), (0,)), ((), ())), precision=highest, preferred_element_type=jnp.float32)
    v_panel = lax.linalg.triangular_solve(l_diag, w_panel - coupling, left_side=True, lower=True, transpose_a=True, unit_diagonal=True)
    x_panel = v_below[pivot]
    x_rest = v_below.at[pivot].set(v_panel)
    return (w_rest, x_panel, x_rest)
```

```python
import functools

import jax
import jax.numpy as jnp
from jax import lax
from jax.experimental import pallas as pl
from jax.experimental.pallas import tpu as pltpu
from jax.sharding import PartitionSpec as P

F32 = jnp.float32
BF16 = jnp.bfloat16
NN = (((1,), (0,)), ((), ()))
TN = (((0,), (0,)), ((), ()))
NT = (((1,), (1,)), ((), ()))
BLOCK = 128
MESH = pl.DeviceIdType.MESH


def split(x):
    high = x.astype(BF16)
    return high, (x - high.astype(F32)).astype(BF16)


def dot(left, right, dims):
    return lax.dot_general(left, right, dims, preferred_element_type=F32)


def dot3(left, right, dims=NN):
    (lh, ll), (rh, rl) = left, right
    return dot(lh, rh, dims) + (dot(lh, rl, dims) + dot(ll, rh, dims))


def inverse(square, upper):
    size = square.shape[0]
    row = lax.broadcasted_iota(jnp.int32, (size, size), 0)
    col = lax.broadcasted_iota(jnp.int32, (size, size), 1)
    eye = jnp.where(row == col, 1.0, 0.0)
    if upper:
        on_diag = jnp.where(row == col, square, 0.0)
        strict = jnp.where(col > row, square, 0.0) / jnp.sum(on_diag, axis=1, keepdims=True)
    else:
        strict = jnp.where(col < row, square, 0.0)
    result = eye - strict
    halves = split(strict)
    power = dot3(halves, halves)
    reach = 2
    while reach < size:
        halves = split(power)
        result = result + dot3(split(result), halves)
        reach *= 2
        if reach < size:
            power = dot3(halves, halves)
    if upper:
        result = result / jnp.sum(on_diag, axis=0, keepdims=True)
    return result


def prep_kernel(pre, u_ref, l_ref, b_ref, lb_ref, vb_ref, piv_ref, pack_ref, extra_ref, coup_ref, pick_ref):
    i = lax.axis_index("prow")
    j = lax.axis_index("pcol")
    cols = u_ref.shape[1]
    chunk = pick_ref.shape[1]
    mine = pl.ds(pl.multiple_of(j * chunk, chunk), chunk)
    ratio = cols // u_ref.shape[0]
    pack_ref[:, :cols] = jnp.where(i // ratio > j, l_ref[...], u_ref[...])
    pack_ref[:, cols:] = b_ref[:, mine]
    extra_ref[...] = l_ref[...]
    if pre:

        @pl.when(i // ratio == j)
        def _():
            at = pl.multiple_of((i % ratio) * BLOCK, BLOCK)
            pack_ref[:, pl.ds(at, BLOCK)] = inverse(u_ref[:, pl.ds(at, BLOCK)], True)
            extra_ref[:, pl.ds(at, BLOCK)] = inverse(l_ref[:, pl.ds(at, BLOCK)], False)

    coup_ref[...] = dot3(split(vb_ref[...]), split(lb_ref[...]), TN)
    pick_rows(i, vb_ref, piv_ref, pick_ref, mine)


def pick_rows(i, vb_ref, piv_ref, pick_ref, mine):
    rows = vb_ref.shape[0]
    total = piv_ref.shape[1]
    local = piv_ref[...] - i * rows
    hot = jnp.where(lax.broadcasted_iota(jnp.int32, (rows, total), 0) == local, 1.0, 0.0).astype(BF16)
    part = vb_ref[:, mine]
    first, _ = split(part)
    second = (part - first.astype(F32)).astype(BF16)
    third = (part - first.astype(F32) - second.astype(F32)).astype(BF16)
    pick_ref[...] = dot(hot, first, TN) + dot(hot, second, TN) + dot(hot, third, TN)


def assemble(n_row, n_col, g_ref, e_ref, uh, ul, lh, ll, bs):
    rows, cols = e_ref.shape[2:]
    chunk = g_ref.shape[3] - cols
    for a in range(n_row):
        for b in range(n_col):
            rs = slice(a * rows, (a + 1) * rows)
            cs_ = slice(b * cols, (b + 1) * cols)
            place = a // (cols // rows)
            if place <= b:
                uh[rs, cs_], ul[rs, cs_] = split(g_ref[a, b, :, :cols])
            if place == b:
                lh[rs, cs_], ll[rs, cs_] = split(e_ref[a, b])
            if place > b:
                lh[rs, cs_], ll[rs, cs_] = split(g_ref[a, b, :, :cols])
            bs[rs, b * chunk : (b + 1) * chunk] = g_ref[a, b, :, cols:]


def first_solve(bs, cs, wh, wl, uh, ul, service):
    for p in range(bs.shape[0] // BLOCK):
        first = p * BLOCK
        sl = slice(first, first + BLOCK)
        rhs = bs[sl, :].T
        if p:
            rhs = rhs - dot3((wh[:, :first], wl[:, :first]), (uh[:first, sl], ul[:first, sl]))
        out = dot3(split(rhs), (uh[sl, sl], ul[sl, sl]))
        cs[:, sl] = out
        wh[:, sl], wl[:, sl] = split(out)
        service(p)


def rest_update(wh, wl, columns, br_ref, wr_ref):
    tile = 256
    for t in range(wr_ref.shape[0] // tile):
        ts = slice(t * tile, (t + 1) * tile)
        wr_ref[ts, :] = br_ref[ts, :] - dot3((wh[...], wl[...]), split(columns(ts))).T


def second_solve(cs, wh, wl, lh, ll):
    total = cs.shape[1]
    for p in reversed(range(total // BLOCK)):
        last = (p + 1) * BLOCK
        sl = slice(p * BLOCK, last)
        rhs = cs[:, sl]
        if last < total:
            rhs = rhs - dot3((wh[:, last:], wl[:, last:]), (lh[last:, sl], ll[last:, sl]))
        wh[:, sl], wl[:, sl] = split(dot3(split(rhs), (lh[sl, sl], ll[sl, sl])))


def interchange(i, wh, wl, vb_ref, piv_ref, xr_ref):
    tile = 256
    all_rows, total = vb_ref.shape[0], piv_ref.shape[1]
    for t in range(all_rows // tile):
        ts = slice(t * tile, (t + 1) * tile)
        local = piv_ref[...] - (i * all_rows + t * tile)
        hot = jnp.where(lax.broadcasted_iota(jnp.int32, (tile, total), 0) == local, 1.0, 0.0)
        used = jnp.sum(hot, axis=1, keepdims=True) > 0.5
        hot = hot.astype(BF16)
        new = dot(hot, wh[...], NT) + dot(hot, wl[...], NT)
        xr_ref[ts, :] = jnp.where(used, new, vb_ref[ts, :])


def unpack_diagonal(packed):
    size = packed.shape[0]
    row = lax.broadcasted_iota(jnp.int32, (size, size), 0)
    col = lax.broadcasted_iota(jnp.int32, (size, size), 1)
    upper = jnp.where(col >= row, packed, 0.0)
    lower = jnp.where(col < row, packed, jnp.where(col == row, 1.0, 0.0))
    return upper, lower


def chain_kernel(n, m, u_hbm, l_hbm, b_hbm, lb_hbm, vb_hbm, up_hbm, br_hbm, piv_ref, wr, xr, xp,
                 u_ref, l_ref, b_ref, lb_ref, gm, gh, gl, bt, bp, cp, cy, cz, pk, py, pz, xparts, gu, hot_ref,
                 uih, uil, lih, lil, rb, rv, ww, vv, aw, av, acc,
                 load_s, ring_s, ring_r, b_s, b_r, cy_s, cy_r, cz_s, cz_r, py_s, py_r, pz_s, pz_r, x_s, x_r,
                 up_s, up_r, row_s, row_r, ag_s, ag_r, sib_s, sib_r):
    i = lax.axis_index("prow")
    j = lax.axis_index("pcol")
    half = n // 2
    rows, cols = u_ref.shape
    share = wr.shape[1] // n
    z, y = i // 2, i % 2
    core = j % 2
    odd = i % 2
    pos = odd * (n - 1 - i // 2) + (1 - odd) * (i // 2)

    def member(at):
        at = (at + n) % n
        back = at // half
        return (1 - back) * 2 * at + back * (2 * (n - 1 - at) + 1)

    right, left = member(pos + 1), member(pos - 1)
    across = (j + m // 2) % m
    beside = j + 1 - 2 * (j % 2)
    over = i + 1 - 2 * (i % 2)

    barrier = pltpu.get_barrier_semaphore()
    for d in range(1, n):
        pl.semaphore_signal(barrier, inc=1, device_id=((i + d) % n, j), device_id_type=MESH)
    for d in range(1, m):
        pl.semaphore_signal(barrier, inc=1, device_id=(i, (j + d) % m), device_id_type=MESH)

    loads = []
    for src, dst in ((u_hbm, u_ref), (l_hbm, l_ref), (b_hbm, b_ref), (lb_hbm, lb_ref), (vb_hbm, xr), (br_hbm, wr), (up_hbm, gu.at[j])):
        loads.append(pltpu.make_async_copy(src, dst, load_s.at[len(loads)]))
        loads[-1].start()

    pending = []

    def guard(cond, action):
        if cond is None:
            action()
        else:
            pl.when(cond)(action)

    def send(src, dst, s_sem, r_sem, to, cond=None):
        copy = pltpu.make_async_remote_copy(src_ref=src, dst_ref=dst, send_sem=s_sem, recv_sem=r_sem, device_id=to, device_id_type=MESH)
        guard(cond, copy.start)
        pending.append((cond, copy))

    def receive(dst, s_sem, r_sem, frm, cond=None):
        copy = pltpu.make_async_remote_copy(src_ref=dst, dst_ref=dst, send_sem=s_sem, recv_sem=r_sem, device_id=frm, device_id_type=MESH)
        guard(cond, copy.wait_recv)

    def reach(way, hop, parity):
        return None if hop < half else parity == way

    def emit(slot, s_sem, r_sem):
        for way, to in ((0, right), (1, left)):
            send(slot(i), slot(i), s_sem.at[way, 0], r_sem.at[way, 0], (to, j))

    def advance(slot, s_sem, r_sem, parity, hop):
        for way, to, frm in ((0, right, left), (1, left, right)):
            row = member(pos - hop) if way == 0 else member(pos + hop)
            receive(slot(row), s_sem.at[way, hop - 1], r_sem.at[way, hop - 1], (frm, j), reach(way, hop, parity))
            if hop < half:
                send(slot(row), slot(row), s_sem.at[way, hop], r_sem.at[way, hop], (to, j), reach(way, hop + 1, parity))

    diagonal = i // 2 == j
    for load in loads[:3]:
        load.wait()
    for h in range(2):
        hs = slice(h * BLOCK, (h + 1) * BLOCK)
        gm[i, h] = jnp.where(i // 2 + (1 - h) * odd > j, l_ref[:, hs], u_ref[:, hs])

    @pl.when(diagonal)
    def _():
        at = pl.multiple_of(odd * BLOCK, BLOCK)
        row = lax.broadcasted_iota(jnp.int32, (BLOCK, BLOCK), 0)
        col = lax.broadcasted_iota(jnp.int32, (BLOCK, BLOCK), 1)
        gm[i, odd] = jnp.where(col >= row, inverse(u_ref[:, pl.ds(at, BLOCK)], True), inverse(l_ref[:, pl.ds(at, BLOCK)], False))
        turned = b_ref[...].T
        for c in range(2):
            for a in range(n):
                first = (c * n + a) * share // 2
                bt[a, c] = turned[first : first + share // 2, :]

    pl.semaphore_wait(barrier, n + m - 2)

    def factor(h):
        return lambda row: gm.at[row, h]

    for h in range(2):
        emit(factor(h), ring_s.at[h], ring_r.at[h])
    for d in range(1, n):
        to = (i + d) % n
        send(bt.at[to], bp.at[odd], b_s.at[d - 1], b_r.at[odd], (to, j), diagonal)

    @pl.when(diagonal)
    def _():
        bp[odd] = bt[i]

    loads[6].wait()
    send(gu.at[j], gu.at[j], up_s.at[0], up_r.at[0], (i, across))
    send(gu.at[j], gu.at[j], up_s.at[1], up_r.at[1], (i, beside))

    loads[3].wait()
    loads[4].wait()
    coup = dot3(split(xr[...]), split(lb_ref[...]), TN)
    for c in range(2):
        for a in range(n):
            first = (c * n + a) * share // 2
            cp[a % 2, a // 2, c] = coup[first : first + share // 2, :]

    def fold_start(part, arrive, y_s, y_r):
        send(part.at[1 - y], arrive, y_s, y_r, (over, j))

    def fold_middle(part, arrive, ends, y_s, y_r, z_s, z_r):
        receive(arrive, y_s, y_r, (over, j))
        part[y] = part[y] + arrive[...]
        for d in range(1, half):
            to = (z + d) % half
            send(part.at[y, to], ends.at[d - 1], z_s.at[d - 1], z_r.at[d - 1], (2 * to + y, j))

    def fold_end(part, ends, z_s, z_r):
        total = part[y, z]
        for d in range(1, half):
            receive(ends.at[d - 1], z_s.at[d - 1], z_r.at[d - 1], (2 * ((z + half - d) % half) + y, j))
            total = total + ends[d - 1]
        return total

    fold_start(cp, cy, cy_s.at[0], cy_r.at[0])
    for h in range(2):
        advance(factor(h), ring_s.at[h], ring_r.at[h], (j + h) % 2, 1)

    tile = 256
    chunk = xp.shape[1] // m
    part = xr[:, pl.ds(pl.multiple_of(j * chunk, chunk), chunk)]
    total = piv_ref.shape[1]
    for t in range(xr.shape[0] // tile):
        ts = slice(t * tile, (t + 1) * tile)
        local = piv_ref[...] - (i * xr.shape[0] + t * tile)
        hot = jnp.where(lax.broadcasted_iota(jnp.int32, (tile, total), 0) == local, 1.0, 0.0)
        hot_ref[ts, :] = hot.astype(BF16)
        used = jnp.sum(hot, axis=1, keepdims=True) > 0.5
        xr[ts, :] = jnp.where(used, 0.0, xr[ts, :])
    for h in range(2):
        advance(factor(h), ring_s.at[h], ring_r.at[h], (j + h) % 2, 2)
    fold_middle(cp, cy, cz, cy_s.at[0], cy_r.at[0], cz_s, cz_r)
    first, _ = split(part)
    second = (part - first.astype(F32)).astype(BF16)
    third = (part - first.astype(F32) - second.astype(F32)).astype(BF16)
    picked = dot(hot_ref[...], first, TN) + dot(hot_ref[...], second, TN) + dot(hot_ref[...], third, TN)
    for a in range(n):
        pk[a % 2, a // 2] = picked[a * rows : (a + 1) * rows, :]
    fold_start(pk, py, py_s.at[0], py_r.at[0])
    for hop in (3, half):
        for h in range(2):
            advance(factor(h), ring_s.at[h], ring_r.at[h], (j + h) % 2, hop)
    fold_middle(pk, py, pz, py_s.at[0], py_r.at[0], pz_s, pz_r)

    for a in range(n):
        for h in range(2):
            at = (slice(a * rows, (a + 1) * rows), slice(h * BLOCK, (h + 1) * BLOCK))
            gh[at], gl[at] = split(gm[a, h])
    a_up, a_low = unpack_diagonal(gm[2 * j, 0])
    d_up, d_low = unpack_diagonal(gm[2 * j + 1, 1])
    one, two = slice(0, BLOCK), slice(BLOCK, 2 * BLOCK)
    uih[...] = jnp.zeros_like(uih)
    uil[...] = jnp.zeros_like(uil)
    lih[...] = jnp.zeros_like(lih)
    lil[...] = jnp.zeros_like(lil)
    uih[one, one], uil[one, one] = split(a_up)
    uih[two, two], uil[two, two] = split(d_up)
    lih[one, one], lil[one, one] = split(a_low)
    lih[two, two], lil[two, two] = split(d_low)
    corner = dot3(split(a_up), split(gm[2 * j, 1]))
    uih[one, two], uil[one, two] = split(-dot3(split(corner), (uih[two, two], uil[two, two])))
    corner = dot3(split(d_low), split(gm[2 * j + 1, 0]))
    lih[two, one], lil[two, one] = split(-dot3(split(corner), (lih[one, one], lil[one, one])))

    for k in range(2):
        owner = 2 * j + k
        receive(bp.at[k], b_s.at[0], b_r.at[k], (owner, j), owner != i)
        for c in range(2):
            rb[c * share // 2 : (c + 1) * share // 2, k * rows : (k + 1) * rows] = bp[k, c]

    def stage(s, forward, out_ref, rhs, inv_h, inv_l):
        lane = 0 if forward else 1

        def later(q):
            return q > s if forward else q < s

        @pl.when(j == s)
        def _():
            if not forward:
                rhs[...] = rhs[...] - fold_end(cp, cz, cz_s, cz_r).reshape(rhs.shape)
            out = dot3(split(rhs[...]), (inv_h[...], inv_l[...]))
            out_ref[s] = out.reshape(out_ref.shape[1:])
            if forward:
                rv[...] = out

        for q in range(m):
            if q == s:
                continue
            if later(q):
                send(out_ref.at[s], out_ref.at[s], row_s.at[lane, s, q], row_r.at[lane, s], (i, q), j == s)
                receive(out_ref.at[s], row_s.at[lane, s, q], row_r.at[lane, s], (i, s), j == q)
            else:
                send(out_ref.at[s, q % 2], out_ref.at[s, q % 2], row_s.at[lane, s, q], row_r.at[lane, s], (i, q), j == s)
                receive(out_ref.at[s, q % 2], row_s.at[lane, s, q], row_r.at[lane, s], (i, s), j == q)

        @pl.when(later(j))
        def _():
            rs = slice(s * cols, (s + 1) * cols)
            rhs[...] = rhs[...] - dot3(split(out_ref[s].reshape(rhs.shape)), (gh[rs, :], gl[rs, :]))

    def ring_of(lane, s):
        whole = (aw, av)[lane]
        return (lambda row: whole.at[s, core, row]), ag_s.at[lane, s], ag_r.at[lane, s]

    def gathered(lane, s):
        whole = (aw, av)[lane]
        receive(whole.at[s, 1 - core], sib_s.at[lane, s], sib_r.at[lane, s], (i, beside))
        halves = split(whole[s].reshape(whole.shape[1] * n * whole.shape[3], cols))
        if lane == 0:
            for t in range(acc.shape[1] // tile):
                ts = slice(t * tile, (t + 1) * tile)
                add = dot3(halves, split(gu[s, :, ts]))
                acc[:, ts] = add if s == 0 else acc[:, ts] + add
        else:
            cs = slice(s * cols, (s + 1) * cols)
            for t in range(xr.shape[0] // tile):
                ts = slice(t * tile, (t + 1) * tile)
                xr[ts, :] += dot(hot_ref[ts, cs], halves[0], NT) + dot(hot_ref[ts, cs], halves[1], NT)

    order = [(0, s) for s in range(m)] + [(1, s) for s in reversed(range(m))]

    def serve(step):
        for hop in range(1, half + 1):
            if 0 <= step - hop < len(order):
                lane, s = order[step - hop]
                slot, s_sem, r_sem = ring_of(lane, s)
                advance(slot, s_sem, r_sem, (j + s) % 2, hop)
                if hop == half:
                    whole = (aw, av)[lane]
                    send(whole.at[s, core], whole.at[s, core], sib_s.at[lane, s], sib_r.at[lane, s], (i, beside))

    waiting = []
    for step in range(len(order) + half + 1):
        if step < len(order):
            lane, s = order[step]
            out_ref = (ww, vv)[lane]
            if lane == 0:
                stage(s, True, out_ref, rb, uih, uil)
            else:
                stage(s, False, out_ref, rv, lih, lil)
            slot, s_sem, r_sem = ring_of(lane, s)
            whole = (aw, av)[lane]
            whole[s, core, i] = out_ref[s, core]
            emit(slot, s_sem, r_sem)
        serve(step)
        if step == 5:
            receive(gu.at[beside], up_s.at[1], up_r.at[1], (i, beside))
        if step == len(order):
            receive(gu.at[across], up_s.at[0], up_r.at[0], (i, across))
            send(gu.at[across], gu.at[across], up_s.at[2], up_r.at[2], (i, beside))
            xparts[j] = fold_end(pk, pz, pz_s, pz_r)
            for d in range(1, m):
                send(xparts.at[j], xparts.at[j], x_s.at[d - 1], x_r.at[d - 1], (i, (j + d) % m))
        if step == len(order) + 1:
            far = (across + 1) - 2 * (across % 2)
            receive(gu.at[far], up_s.at[2], up_r.at[2], (i, beside))
        if 0 <= step - half - 1 < len(order):
            waiting.append(order[step - half - 1])
        while waiting and (waiting[0][0] == 1 or step > len(order)):
            gathered(*waiting.pop(0))
        if step == len(order) + 2:
            loads[5].wait()
            for t in range(wr.shape[0] // tile):
                ts = slice(t * tile, (t + 1) * tile)
                wr[ts, :] = wr[ts, :] - acc[:, ts].T
    for d in range(1, m):
        frm = (j - d + m) % m
        receive(xparts.at[frm], x_s.at[d - 1], x_r.at[d - 1], (i, frm))
    for q in range(m):
        xp[:, q * chunk : (q + 1) * chunk] = xparts[q]
    for cond, copy in pending:
        guard(cond, copy.wait_send)


def store_kernel(w_ref, p_ref, x_ref, w_out, p_out, x_out, sems):
    copies = [pltpu.make_async_copy(a, b, sems.at[k]) for k, (a, b) in enumerate(((w_ref, w_out), (x_ref, x_out), (p_ref, p_out)))]
    for copy in copies:
        copy.start()
    for copy in copies:
        copy.wait()


def main_kernel(pre, g_ref, e_ref, c_ref, up_ref, br_ref, vb_ref, piv_ref, wr_ref, xr_ref, uh, ul, lh, ll, bs, cs, wh, wl):
    n_row, n_col, crow, cols = c_ref.shape
    assemble(n_row, n_col, g_ref, e_ref, uh, ul, lh, ll, bs)
    if not pre:
        for p in range(uh.shape[0] // BLOCK):
            sl = slice(p * BLOCK, (p + 1) * BLOCK)
            uh[sl, sl], ul[sl, sl] = split(inverse(uh[sl, sl].astype(F32) + ul[sl, sl].astype(F32), True))
            lh[sl, sl], ll[sl, sl] = split(inverse(lh[sl, sl].astype(F32) + ll[sl, sl].astype(F32), False))
    first_solve(bs, cs, wh, wl, uh, ul, lambda p: None)
    for a in range(n_row):
        for b in range(n_col):
            cs[a * crow : (a + 1) * crow, b * cols : (b + 1) * cols] -= c_ref[a, b]
    rest_update(wh, wl, lambda ts: up_ref[:, ts], br_ref, wr_ref)
    second_solve(cs, wh, wl, lh, ll)
    interchange(lax.axis_index("prow"), wh, wl, vb_ref, piv_ref, xr_ref)


def body(n_row, n_col, b_panel, b_rest, u_diag, u_panel, l_diag, l_below, v_below, pivot):
    rows, cols = u_diag.shape
    total, rhs = pivot.shape[0], b_panel.shape[1]
    chunk = rhs // n_col
    pre = rows == BLOCK
    piv = pivot[None, :]
    vm = pl.BlockSpec(memory_space=pltpu.VMEM)
    params = pltpu.CompilerParams(vmem_limit_bytes=56 << 20)
    halves = [pltpu.VMEM((total, total), BF16)] * 4
    halves += [pltpu.VMEM((total, rhs), F32), pltpu.VMEM((rhs, total), F32)]
    halves += [pltpu.VMEM((rhs, total), BF16)] * 2
    if pre and n_row == 8 and n_col == 4:
        half, share = n_row // 2, rhs // n_row
        anywhere = pl.BlockSpec(memory_space=pl.ANY)
        blocks = [
            pltpu.VMEM((rows, cols), F32),
            pltpu.VMEM((rows, cols), F32),
            pltpu.VMEM((rows, rhs), F32),
            pltpu.VMEM(l_below.shape, F32),
            pltpu.VMEM((n_row, 2, rows, BLOCK), F32),
            pltpu.VMEM((total, cols), BF16),
            pltpu.VMEM((total, cols), BF16),
            pltpu.VMEM((n_row, 2, share // 2, rows), F32),
            pltpu.VMEM((2, 2, share // 2, rows), F32),
            pltpu.VMEM((2, half, 2, share // 2, cols), F32),
            pltpu.VMEM((half, 2, share // 2, cols), F32),
            pltpu.VMEM((half - 1, 2, share // 2, cols), F32),
            pltpu.VMEM((2, half, rows, chunk), F32),
            pltpu.VMEM((half, rows, chunk), F32),
            pltpu.VMEM((half - 1, rows, chunk), F32),
            pltpu.VMEM((n_col, rows, chunk), F32),
            pltpu.VMEM((n_col,) + u_panel.shape, F32),
            pltpu.VMEM((v_below.shape[0], total), BF16),
        ]
        blocks += [pltpu.VMEM((cols, cols), BF16)] * 4
        blocks += [pltpu.VMEM((share, cols), F32)] * 2
        blocks += [pltpu.VMEM((n_col, 2, share // 2, cols), F32)] * 2
        blocks += [pltpu.VMEM((n_col, 2, n_row, share // 2, cols), F32)] * 2
        blocks += [pltpu.VMEM((rhs, u_panel.shape[1]), F32)]
        counts = [(7,), (2, 2, half), (2, 2, half), (n_row - 1,), (2,), (1,), (1,), (half - 1,), (half - 1,), (1,), (1,), (half - 1,), (half - 1,)]
        counts += [(n_col - 1,)] * 2 + [(3,)] * 2 + [(2, n_col, n_col), (2, n_col)] + [(2, n_col, 2, half)] * 2 + [(2, n_col)] * 2
        w_rest, x_rest, x_panel = pl.pallas_call(
            functools.partial(chain_kernel, n_row, n_col),
            out_shape=(
                jax.ShapeDtypeStruct(b_rest.shape, F32),
                jax.ShapeDtypeStruct(v_below.shape, F32),
                jax.ShapeDtypeStruct((rows, rhs), F32),
            ),
            in_specs=[anywhere] * 7 + [vm],
            out_specs=(vm,) * 3,
            scratch_shapes=blocks + [pltpu.SemaphoreType.DMA(shape) for shape in counts],
            compiler_params=pltpu.CompilerParams(vmem_limit_bytes=40 << 20, collective_id=0, has_side_effects=True),
        )(u_diag, l_diag, b_panel, l_below, v_below, u_panel, b_rest, piv)
        return pl.pallas_call(
            store_kernel,
            out_shape=(
                jax.ShapeDtypeStruct(b_rest.shape, F32),
                jax.ShapeDtypeStruct((rows, rhs), F32),
                jax.ShapeDtypeStruct(v_below.shape, F32),
            ),
            in_specs=[vm] * 3,
            out_specs=(anywhere,) * 3,
            scratch_shapes=[pltpu.SemaphoreType.DMA((3,))],
            compiler_params=pltpu.CompilerParams(vmem_limit_bytes=8 << 20),
        )(w_rest, x_panel, x_rest)
    pack, extra, coup, pick = pl.pallas_call(
        functools.partial(prep_kernel, pre),
        out_shape=(
            jax.ShapeDtypeStruct((rows, cols + chunk), F32),
            jax.ShapeDtypeStruct((rows, cols), F32),
            jax.ShapeDtypeStruct((rhs, cols), F32),
            jax.ShapeDtypeStruct((total, chunk), F32),
        ),
        in_specs=[vm] * 6,
        out_specs=(vm,) * 4,
        compiler_params=params,
    )(u_diag, l_diag, b_panel, l_below, v_below, piv)

    def everywhere(piece):
        return lax.all_gather(piece, ("prow", "pcol"), axis=0).reshape((n_row, n_col) + piece.shape)

    upan = lax.all_gather(u_panel, "pcol", axis=0, tiled=True)
    csum = lax.psum_scatter(coup, "prow", scatter_dimension=0, tiled=True)
    xsum = lax.psum_scatter(pick, "prow", scatter_dimension=0, tiled=True)
    x_panel = lax.all_gather(xsum, "pcol", axis=1, tiled=True)
    w_rest, x_rest = pl.pallas_call(
        functools.partial(main_kernel, pre),
        out_shape=(jax.ShapeDtypeStruct(b_rest.shape, F32), jax.ShapeDtypeStruct(v_below.shape, F32)),
        in_specs=[vm] * 7,
        out_specs=(vm, vm),
        scratch_shapes=halves,
        compiler_params=params,
    )(everywhere(pack), everywhere(extra), everywhere(csum), upan, b_rest, v_below, piv)
    return w_rest, x_panel, x_rest


def solution(mesh):
    in_specs = (
        P("prow", None),
        P("prow", None),
        P("prow", "pcol"),
        P("pcol", "prow"),
        P("prow", "pcol"),
        P("prow", "pcol"),
        P("prow", None),
        P(),
    )
    out_specs = (P("prow", None), P("prow", None), P("prow", None))
    step = functools.partial(body, mesh.shape["prow"], mesh.shape["pcol"])
    return jax.shard_map(step, mesh=mesh, in_specs=in_specs, out_specs=out_specs, check_vma=False)
```

```python
import functools

import jax
import jax.numpy as jnp
from jax import lax
from jax.experimental import pallas as pl
from jax.experimental.pallas import tpu as pltpu
from jax.sharding import PartitionSpec as P

F32 = jnp.float32
BF16 = jnp.bfloat16
NN = (((1,), (0,)), ((), ()))
TN = (((0,), (0,)), ((), ()))
NT = (((1,), (1,)), ((), ()))
BLOCK = 128
MESH = pl.DeviceIdType.MESH


def split(x):
    high = x.astype(BF16)
    return high, (x - high.astype(F32)).astype(BF16)


def dot(left, right, dims):
    return lax.dot_general(left, right, dims, preferred_element_type=F32)


def dot3(left, right, dims=NN):
    (lh, ll), (rh, rl) = left, right
    return dot(lh, rh, dims) + (dot(lh, rl, dims) + dot(ll, rh, dims))


def inverse(square, upper):
    size = square.shape[0]
    row = lax.broadcasted_iota(jnp.int32, (size, size), 0)
    col = lax.broadcasted_iota(jnp.int32, (size, size), 1)
    eye = jnp.where(row == col, 1.0, 0.0)
    if upper:
        on_diag = jnp.where(row == col, square, 0.0)
        strict = jnp.where(col > row, square, 0.0) / jnp.sum(on_diag, axis=1, keepdims=True)
    else:
        strict = jnp.where(col < row, square, 0.0)
    result = eye - strict
    halves = split(strict)
    power = dot3(halves, halves)
    reach = 2
    while reach < size:
        halves = split(power)
        result = result + dot3(split(result), halves)
        reach *= 2
        if reach < size:
            power = dot3(halves, halves)
    if upper:
        result = result / jnp.sum(on_diag, axis=0, keepdims=True)
    return result


def prep_kernel(pre, u_ref, l_ref, b_ref, lb_ref, vb_ref, piv_ref, pack_ref, extra_ref, coup_ref, pick_ref):
    i = lax.axis_index("prow")
    j = lax.axis_index("pcol")
    cols = u_ref.shape[1]
    chunk = pick_ref.shape[1]
    mine = pl.ds(pl.multiple_of(j * chunk, chunk), chunk)
    ratio = cols // u_ref.shape[0]
    pack_ref[:, :cols] = jnp.where(i // ratio > j, l_ref[...], u_ref[...])
    pack_ref[:, cols:] = b_ref[:, mine]
    extra_ref[...] = l_ref[...]
    if pre:

        @pl.when(i // ratio == j)
        def _():
            at = pl.multiple_of((i % ratio) * BLOCK, BLOCK)
            pack_ref[:, pl.ds(at, BLOCK)] = inverse(u_ref[:, pl.ds(at, BLOCK)], True)
            extra_ref[:, pl.ds(at, BLOCK)] = inverse(l_ref[:, pl.ds(at, BLOCK)], False)

    coup_ref[...] = dot3(split(vb_ref[...]), split(lb_ref[...]), TN)
    pick_rows(i, vb_ref, piv_ref, pick_ref, mine)


def pick_rows(i, vb_ref, piv_ref, pick_ref, mine):
    rows = vb_ref.shape[0]
    total = piv_ref.shape[1]
    local = piv_ref[...] - i * rows
    hot = jnp.where(lax.broadcasted_iota(jnp.int32, (rows, total), 0) == local, 1.0, 0.0).astype(BF16)
    part = vb_ref[:, mine]
    first, _ = split(part)
    second = (part - first.astype(F32)).astype(BF16)
    third = (part - first.astype(F32) - second.astype(F32)).astype(BF16)
    pick_ref[...] = dot(hot, first, TN) + dot(hot, second, TN) + dot(hot, third, TN)


def assemble(n_row, n_col, g_ref, e_ref, uh, ul, lh, ll, bs):
    rows, cols = e_ref.shape[2:]
    chunk = g_ref.shape[3] - cols
    for a in range(n_row):
        for b in range(n_col):
            rs = slice(a * rows, (a + 1) * rows)
            cs_ = slice(b * cols, (b + 1) * cols)
            place = a // (cols // rows)
            if place <= b:
                uh[rs, cs_], ul[rs, cs_] = split(g_ref[a, b, :, :cols])
            if place == b:
                lh[rs, cs_], ll[rs, cs_] = split(e_ref[a, b])
            if place > b:
                lh[rs, cs_], ll[rs, cs_] = split(g_ref[a, b, :, :cols])
            bs[rs, b * chunk : (b + 1) * chunk] = g_ref[a, b, :, cols:]


def first_solve(bs, cs, wh, wl, uh, ul, service):
    for p in range(bs.shape[0] // BLOCK):
        first = p * BLOCK
        sl = slice(first, first + BLOCK)
        rhs = bs[sl, :].T
        if p:
            rhs = rhs - dot3((wh[:, :first], wl[:, :first]), (uh[:first, sl], ul[:first, sl]))
        out = dot3(split(rhs), (uh[sl, sl], ul[sl, sl]))
        cs[:, sl] = out
        wh[:, sl], wl[:, sl] = split(out)
        service(p)


def rest_update(wh, wl, columns, br_ref, wr_ref):
    tile = 256
    for t in range(wr_ref.shape[0] // tile):
        ts = slice(t * tile, (t + 1) * tile)
        wr_ref[ts, :] = br_ref[ts, :] - dot3((wh[...], wl[...]), split(columns(ts))).T


def second_solve(cs, wh, wl, lh, ll):
    total = cs.shape[1]
    for p in reversed(range(total // BLOCK)):
        last = (p + 1) * BLOCK
        sl = slice(p * BLOCK, last)
        rhs = cs[:, sl]
        if last < total:
            rhs = rhs - dot3((wh[:, last:], wl[:, last:]), (lh[last:, sl], ll[last:, sl]))
        wh[:, sl], wl[:, sl] = split(dot3(split(rhs), (lh[sl, sl], ll[sl, sl])))


def interchange(i, wh, wl, vb_ref, piv_ref, xr_ref):
    tile = 256
    all_rows, total = vb_ref.shape[0], piv_ref.shape[1]
    for t in range(all_rows // tile):
        ts = slice(t * tile, (t + 1) * tile)
        local = piv_ref[...] - (i * all_rows + t * tile)
        hot = jnp.where(lax.broadcasted_iota(jnp.int32, (tile, total), 0) == local, 1.0, 0.0)
        used = jnp.sum(hot, axis=1, keepdims=True) > 0.5
        hot = hot.astype(BF16)
        new = dot(hot, wh[...], NT) + dot(hot, wl[...], NT)
        xr_ref[ts, :] = jnp.where(used, new, vb_ref[ts, :])


def unpack_diagonal(packed):
    size = packed.shape[0]
    row = lax.broadcasted_iota(jnp.int32, (size, size), 0)
    col = lax.broadcasted_iota(jnp.int32, (size, size), 1)
    upper = jnp.where(col >= row, packed, 0.0)
    lower = jnp.where(col < row, packed, jnp.where(col == row, 1.0, 0.0))
    return upper, lower


def chain_kernel(n, m, u_hbm, l_hbm, b_hbm, lb_hbm, vb_hbm, up_hbm, br_hbm, piv_hbm, wr, xr, xp,
                 piv_ref, part_ref, u_ref, l_ref, b_ref, lb_ref, gm, gh, gl, bt, bp, cp, cy, cz, pk, py, pz, xparts, gu, hot_ref,
                 uih, uil, lih, lil, rb, rv, ww, vv, aw, av, acc,
                 load_s, ring_s, ring_r, b_s, b_r, cy_s, cy_r, cz_s, cz_r, py_s, py_r, pz_s, pz_r, x_s, x_r,
                 up_s, up_r, row_s, row_r, agz_s, agz_r, agy_s, agy_r, sib_s, sib_r):
    i = lax.axis_index("prow")
    j = lax.axis_index("pcol")
    half = n // 2
    rows, cols = u_ref.shape
    share = wr.shape[1] // n
    z, y = i // 2, i % 2
    core = j % 2
    odd = i % 2
    pos = odd * (n - 1 - i // 2) + (1 - odd) * (i // 2)

    def member(at):
        at = (at + n) % n
        back = at // half
        return (1 - back) * 2 * at + back * (2 * (n - 1 - at) + 1)

    right, left = member(pos + 1), member(pos - 1)
    across = (j + m // 2) % m
    beside = j + 1 - 2 * (j % 2)
    over = i + 1 - 2 * (i % 2)

    barrier = pltpu.get_barrier_semaphore()
    for d in range(1, n):
        pl.semaphore_signal(barrier, inc=1, device_id=((i + d) % n, j), device_id_type=MESH)
    for d in range(1, m):
        pl.semaphore_signal(barrier, inc=1, device_id=(i, (j + d) % m), device_id_type=MESH)

    loads = []
    for src, dst in ((u_hbm, u_ref), (l_hbm, l_ref), (b_hbm, b_ref), (lb_hbm, lb_ref), (vb_hbm, xr), (br_hbm, wr), (up_hbm, gu.at[j]), (piv_hbm, piv_ref)):
        loads.append(pltpu.make_async_copy(src, dst, load_s.at[len(loads)]))
        loads[-1].start()

    pending = []

    def guard(cond, action):
        if cond is None:
            action()
        else:
            pl.when(cond)(action)

    def send(src, dst, s_sem, r_sem, to, cond=None):
        copy = pltpu.make_async_remote_copy(src_ref=src, dst_ref=dst, send_sem=s_sem, recv_sem=r_sem, device_id=to, device_id_type=MESH)
        guard(cond, copy.start)
        pending.append((cond, copy))

    def receive(dst, s_sem, r_sem, frm, cond=None):
        copy = pltpu.make_async_remote_copy(src_ref=dst, dst_ref=dst, send_sem=s_sem, recv_sem=r_sem, device_id=frm, device_id_type=MESH)
        guard(cond, copy.wait_recv)

    def reach(way, hop, parity):
        return None if hop < half else parity == way

    def emit(slot, s_sem, r_sem):
        for way, to in ((0, right), (1, left)):
            send(slot(i), slot(i), s_sem.at[way, 0], r_sem.at[way, 0], (to, j))

    def advance(slot, s_sem, r_sem, parity, hop):
        for way, to, frm in ((0, right, left), (1, left, right)):
            row = member(pos - hop) if way == 0 else member(pos + hop)
            receive(slot(row), s_sem.at[way, hop - 1], r_sem.at[way, hop - 1], (frm, j), reach(way, hop, parity))
            if hop < half:
                send(slot(row), slot(row), s_sem.at[way, hop], r_sem.at[way, hop], (to, j), reach(way, hop + 1, parity))

    diagonal = i // 2 == j
    for load in loads[:3]:
        load.wait()
    for h in range(2):
        hs = slice(h * BLOCK, (h + 1) * BLOCK)
        gm[i, h] = jnp.where(i // 2 + (1 - h) * odd > j, l_ref[:, hs], u_ref[:, hs])

    @pl.when(diagonal)
    def _():
        at = pl.multiple_of(odd * BLOCK, BLOCK)
        row = lax.broadcasted_iota(jnp.int32, (BLOCK, BLOCK), 0)
        col = lax.broadcasted_iota(jnp.int32, (BLOCK, BLOCK), 1)
        gm[i, odd] = jnp.where(col >= row, inverse(u_ref[:, pl.ds(at, BLOCK)], True), inverse(l_ref[:, pl.ds(at, BLOCK)], False))
        turned = b_ref[...].T
        for c in range(2):
            for a in range(n):
                first = (c * n + a % 2 * half + a // 2) * share // 2
                bt[a, c] = turned[first : first + share // 2, :]

    pl.semaphore_wait(barrier, n + m - 2)

    def factor(h):
        return lambda row: gm.at[row, h]

    for h in range(2):
        emit(factor(h), ring_s.at[h], ring_r.at[h])
    for d in range(1, n):
        to = (i + d) % n
        send(bt.at[to], bp.at[odd], b_s.at[d - 1], b_r.at[odd], (to, j), diagonal)

    @pl.when(diagonal)
    def _():
        bp[odd] = bt[i]

    loads[6].wait()
    send(gu.at[j], gu.at[j], up_s.at[0], up_r.at[0], (i, across))
    send(gu.at[j], gu.at[j], up_s.at[1], up_r.at[1], (i, beside))

    def fold_start(part, arrive, y_s, y_r):
        send(part.at[1 - y], arrive, y_s, y_r, (over, j))

    def fold_middle(part, arrive, ends, y_s, y_r, z_s, z_r):
        receive(arrive, y_s, y_r, (over, j))
        part[y] = part[y] + arrive[...]
        for d in range(1, half):
            to = (z + d) % half
            send(part.at[y, to], ends.at[d - 1], z_s.at[d - 1], z_r.at[d - 1], (2 * to + y, j))

    def fold_end(part, ends, z_s, z_r):
        total = part[y, z]
        for d in range(1, half):
            receive(ends.at[d - 1], z_s.at[d - 1], z_r.at[d - 1], (2 * ((z + half - d) % half) + y, j))
            total = total + ends[d - 1]
        return total

    loads[3].wait()
    loads[4].wait()
    coup = dot3(split(xr[...]), split(lb_ref[...]), TN)
    for c in range(2):
        for a in range(n):
            first = (c * n + a % 2 * half + a // 2) * share // 2
            cp[a % 2, a // 2, c] = coup[first : first + share // 2, :]
    fold_start(cp, cy, cy_s.at[0], cy_r.at[0])
    for h in range(2):
        advance(factor(h), ring_s.at[h], ring_r.at[h], (j + h) % 2, 1)

    tile = 256
    chunk = xp.shape[1] // m
    part_ref[...] = xr[:, pl.ds(pl.multiple_of(j * chunk, chunk), chunk)]
    total = piv_ref.shape[1]
    loads[7].wait()
    for t in range(xr.shape[0] // tile):
        ts = slice(t * tile, (t + 1) * tile)
        local = piv_ref[...] - (i * xr.shape[0] + t * tile)
        hot = jnp.where(lax.broadcasted_iota(jnp.int32, (tile, total), 0) == local, 1.0, 0.0)
        hot_ref[ts, :] = hot.astype(BF16)
        used = jnp.sum(hot, axis=1, keepdims=True) > 0.5
        xr[ts, :] = jnp.where(used, 0.0, xr[ts, :])
    for h in range(2):
        advance(factor(h), ring_s.at[h], ring_r.at[h], (j + h) % 2, 2)
    for hop in (3, half):
        for h in range(2):
            advance(factor(h), ring_s.at[h], ring_r.at[h], (j + h) % 2, hop)

    for a in range(n):
        for h in range(2):
            at = (slice(a * rows, (a + 1) * rows), slice(h * BLOCK, (h + 1) * BLOCK))
            gh[at], gl[at] = split(gm[a, h])
    a_up, a_low = unpack_diagonal(gm[2 * j, 0])
    d_up, d_low = unpack_diagonal(gm[2 * j + 1, 1])
    one, two = slice(0, BLOCK), slice(BLOCK, 2 * BLOCK)
    uih[...] = jnp.zeros_like(uih)
    uil[...] = jnp.zeros_like(uil)
    lih[...] = jnp.zeros_like(lih)
    lil[...] = jnp.zeros_like(lil)
    uih[one, one], uil[one, one] = split(a_up)
    uih[two, two], uil[two, two] = split(d_up)
    lih[one, one], lil[one, one] = split(a_low)
    lih[two, two], lil[two, two] = split(d_low)
    corner = dot3(split(a_up), split(gm[2 * j, 1]))
    uih[one, two], uil[one, two] = split(-dot3(split(corner), (uih[two, two], uil[two, two])))
    corner = dot3(split(d_low), split(gm[2 * j + 1, 0]))
    lih[two, one], lil[two, one] = split(-dot3(split(corner), (lih[one, one], lil[one, one])))

    for k in range(2):
        owner = 2 * j + k
        receive(bp.at[k], b_s.at[0], b_r.at[k], (owner, j), owner != i)
        for c in range(2):
            rb[c * share // 2 : (c + 1) * share // 2, k * rows : (k + 1) * rows] = bp[k, c]

    def stage(s, forward, out_ref, rhs, inv_h, inv_l):
        lane = 0 if forward else 1

        def later(q):
            return q > s if forward else q < s

        @pl.when(j == s)
        def _():
            if not forward:
                rhs[...] = rhs[...] - fold_end(cp, cz, cz_s, cz_r).reshape(rhs.shape)
            out = dot3(split(rhs[...]), (inv_h[...], inv_l[...]))
            out_ref[s] = out.reshape(out_ref.shape[1:])
            if forward:
                rv[...] = out

        for q in list(range(s + 1, m)) + list(range(s - 1, -1, -1)) if forward else list(range(s - 1, -1, -1)) + list(range(s + 1, m)):
            if later(q):
                send(out_ref.at[s], out_ref.at[s], row_s.at[lane, s, q], row_r.at[lane, s], (i, q), j == s)
                receive(out_ref.at[s], row_s.at[lane, s, q], row_r.at[lane, s], (i, s), j == q)
            else:
                send(out_ref.at[s, q % 2], out_ref.at[s, q % 2], row_s.at[lane, s, q], row_r.at[lane, s], (i, q), j == s)
                receive(out_ref.at[s, q % 2], row_s.at[lane, s, q], row_r.at[lane, s], (i, s), j == q)

        @pl.when(later(j))
        def _():
            rs = slice(s * cols, (s + 1) * cols)
            rhs[...] = rhs[...] - dot3(split(out_ref[s].reshape(rhs.shape)), (gh[rs, :], gl[rs, :]))

    def line(way, k):
        reached = z >= k if way == 0 else z + k < half
        return reached, (z + (half - k if way == 0 else k)) % half

    def spread(lane, s, direct=False):
        whole = (aw, av)[lane]
        own = whole.at[s, core, y, z]
        whole[s, core, y, z] = (ww, vv)[lane][s, core]
        if direct:
            for d in range(1, half):
                send(own, own, agz_s.at[lane, s, 0, d - 1], agz_r.at[lane, s, 0, d - 1], (2 * ((z + d) % half) + y, j))
        else:
            for way in (0, 1):
                there, to = line(1 - way, 1)
                send(own, own, agz_s.at[lane, s, way, 0], agz_r.at[lane, s, way, 0], (2 * to + y, j), there)
        send(own, own, agy_s.at[lane, s, 0, 0], agy_r.at[lane, s, 0, 0], (over, j))

    def onward(lane, s, k):
        for way in (0, 1):
            reached, frm = line(way, k)
            there, to = line(1 - way, 1)
            slot = (aw, av)[lane].at[s, core, y, frm]
            receive(slot, agz_s.at[lane, s, way, k - 1], agz_r.at[lane, s, way, k - 1], (2 * ((z + (half - 1 if way == 0 else 1)) % half) + y, j), reached)
            if k < half - 1:
                send(slot, slot, agz_s.at[lane, s, way, k], agz_r.at[lane, s, way, k], (2 * to + y, j), reached & there)
            send(slot, slot, agy_s.at[lane, s, way, k], agy_r.at[lane, s, way, k], (over, j), reached)

    def onward_direct(lane, s):
        for d in range(1, half):
            frm = (z + half - d) % half
            slot = (aw, av)[lane].at[s, core, y, frm]
            receive(slot, agz_s.at[lane, s, 0, d - 1], agz_r.at[lane, s, 0, d - 1], (2 * frm + y, j))
            send(slot, slot, agy_s.at[lane, s, 0, d], agy_r.at[lane, s, 0, d], (over, j))

    def complete(lane, s, direct=False):
        whole = (aw, av)[lane]
        receive(whole.at[s, core, 1 - y, z], agy_s.at[lane, s, 0, 0], agy_r.at[lane, s, 0, 0], (over, j))
        for d in range(1, half):
            if direct:
                receive(whole.at[s, core, 1 - y, (z + half - d) % half], agy_s.at[lane, s, 0, d], agy_r.at[lane, s, 0, d], (over, j))
            else:
                for way in (0, 1):
                    reached, frm = line(way, d)
                    receive(whole.at[s, core, 1 - y, frm], agy_s.at[lane, s, way, d], agy_r.at[lane, s, way, d], (over, j), reached)
        send(whole.at[s, core], whole.at[s, core], sib_s.at[lane, s], sib_r.at[lane, s], (i, beside))

    def gathered(lane, s):
        whole = (aw, av)[lane]
        receive(whole.at[s, 1 - core], sib_s.at[lane, s], sib_r.at[lane, s], (i, beside))
        halves = split(whole[s].reshape(2 * n * share // 2, cols))
        if lane == 0:
            for t in range(acc.shape[1] // tile):
                ts = slice(t * tile, (t + 1) * tile)
                add = dot3(halves, split(gu[s, :, ts]))
                acc[:, ts] = add if s == 0 else acc[:, ts] + add
        else:
            cs = slice(s * cols, (s + 1) * cols)
            for t in range(xr.shape[0] // tile):
                ts = slice(t * tile, (t + 1) * tile)
                xr[ts, :] += dot(hot_ref[ts, cs], halves[0], NT) + dot(hot_ref[ts, cs], halves[1], NT)

    def fold_x():
        xparts[j] = fold_end(pk, pz, pz_s, pz_r)
        for d in range(1, m):
            send(xparts.at[j], xparts.at[j], x_s.at[d - 1], x_r.at[d - 1], (i, (j + d) % m))

    def near_u():
        receive(gu.at[beside], up_s.at[1], up_r.at[1], (i, beside))

    def cross_u():
        receive(gu.at[across], up_s.at[0], up_r.at[0], (i, across))
        send(gu.at[across], gu.at[across], up_s.at[2], up_r.at[2], (i, beside))

    def far_u():
        far = (across + 1) - 2 * (across % 2)
        receive(gu.at[far], up_s.at[2], up_r.at[2], (i, beside))

    def finish_w():
        loads[5].wait()
        for t in range(wr.shape[0] // tile):
            ts = slice(t * tile, (t + 1) * tile)
            wr[ts, :] = wr[ts, :] - acc[:, ts].T

    def pick():
        part = part_ref[...]
        first, _ = split(part)
        second = (part - first.astype(F32)).astype(BF16)
        third = (part - first.astype(F32) - second.astype(F32)).astype(BF16)
        picked = dot(hot_ref[...], first, TN) + dot(hot_ref[...], second, TN) + dot(hot_ref[...], third, TN)
        for a in range(n):
            pk[a % 2, a // 2] = picked[a * rows : (a + 1) * rows, :]

    W, V = 0, 1
    order = [(W, s) for s in range(m)] + [(V, s) for s in reversed(range(m))]
    last = order[-1]

    def solve(step):
        lane, s = order[step]
        if lane == 0:
            stage(s, True, ww, rb, uih, uil)
        else:
            stage(s, False, vv, rv, lih, lil)
        spread(lane, s, order[step] == last)

    late = len(order) - 1

    def serve(step):
        for k in range(1, half):
            for at in range(late):
                if when(at, k) == step:
                    onward(*order[at], k)
        for at in range(late):
            if when(at, half) == step:
                complete(*order[at])

    def when(at, k):
        step = at
        for _ in range(k):
            step += 2 if step < late else 1
        return step

    fold_middle(cp, cy, cz, cy_s.at[0], cy_r.at[0], cz_s, cz_r)
    pl.when(j >= m // 2)(pick)
    for step in range(len(order)):
        solve(step)
        serve(step)
        if step == 2:
            pl.when(j < m // 2)(pick)
            fold_start(pk, py, py_s.at[0], py_r.at[0])
        if step == 3:
            near_u()
        if step == 5:
            fold_middle(pk, py, pz, py_s.at[0], py_r.at[0], pz_s, pz_r)
    serve(8)
    cross_u()
    onward_direct(*last)
    serve(9)
    fold_x()
    far_u()
    gathered(W, 0)
    serve(10)
    serve(11)
    complete(*last, True)
    gathered(W, 1)
    gathered(V, 3)
    gathered(V, 2)
    gathered(V, 1)
    gathered(W, 2)
    gathered(W, 3)
    gathered(*last)
    finish_w()
    for d in range(1, m):
        frm = (j - d + m) % m
        receive(xparts.at[frm], x_s.at[d - 1], x_r.at[d - 1], (i, frm))
    for q in range(m):
        xp[:, q * chunk : (q + 1) * chunk] = xparts[q]
    for cond, copy in pending:
        guard(cond, copy.wait_send)


def store_kernel(w_ref, p_ref, x_ref, w_out, p_out, x_out, sems):
    copies = [pltpu.make_async_copy(a, b, sems.at[k]) for k, (a, b) in enumerate(((w_ref, w_out), (x_ref, x_out), (p_ref, p_out)))]
    for copy in copies:
        copy.start()
    for copy in copies:
        copy.wait()


def main_kernel(pre, g_ref, e_ref, c_ref, up_ref, br_ref, vb_ref, piv_ref, wr_ref, xr_ref, uh, ul, lh, ll, bs, cs, wh, wl):
    n_row, n_col, crow, cols = c_ref.shape
    assemble(n_row, n_col, g_ref, e_ref, uh, ul, lh, ll, bs)
    if not pre:
        for p in range(uh.shape[0] // BLOCK):
            sl = slice(p * BLOCK, (p + 1) * BLOCK)
            uh[sl, sl], ul[sl, sl] = split(inverse(uh[sl, sl].astype(F32) + ul[sl, sl].astype(F32), True))
            lh[sl, sl], ll[sl, sl] = split(inverse(lh[sl, sl].astype(F32) + ll[sl, sl].astype(F32), False))
    first_solve(bs, cs, wh, wl, uh, ul, lambda p: None)
    for a in range(n_row):
        for b in range(n_col):
            cs[a * crow : (a + 1) * crow, b * cols : (b + 1) * cols] -= c_ref[a, b]
    rest_update(wh, wl, lambda ts: up_ref[:, ts], br_ref, wr_ref)
    second_solve(cs, wh, wl, lh, ll)
    interchange(lax.axis_index("prow"), wh, wl, vb_ref, piv_ref, xr_ref)


def body(n_row, n_col, b_panel, b_rest, u_diag, u_panel, l_diag, l_below, v_below, pivot):
    rows, cols = u_diag.shape
    total, rhs = pivot.shape[0], b_panel.shape[1]
    chunk = rhs // n_col
    pre = rows == BLOCK
    piv = pivot[None, :]
    vm = pl.BlockSpec(memory_space=pltpu.VMEM)
    params = pltpu.CompilerParams(vmem_limit_bytes=56 << 20)
    halves = [pltpu.VMEM((total, total), BF16)] * 4
    halves += [pltpu.VMEM((total, rhs), F32), pltpu.VMEM((rhs, total), F32)]
    halves += [pltpu.VMEM((rhs, total), BF16)] * 2
    if pre and n_row == 8 and n_col == 4:
        half, share = n_row // 2, rhs // n_row
        anywhere = pl.BlockSpec(memory_space=pltpu.HBM)
        blocks = [
            pltpu.VMEM(piv.shape, jnp.int32),
            pltpu.VMEM((v_below.shape[0], chunk), F32),
            pltpu.VMEM((rows, cols), F32),
            pltpu.VMEM((rows, cols), F32),
            pltpu.VMEM((rows, rhs), F32),
            pltpu.VMEM(l_below.shape, F32),
            pltpu.VMEM((n_row, 2, rows, BLOCK), F32),
            pltpu.VMEM((total, cols), BF16),
            pltpu.VMEM((total, cols), BF16),
            pltpu.VMEM((n_row, 2, share // 2, rows), F32),
            pltpu.VMEM((2, 2, share // 2, rows), F32),
            pltpu.VMEM((2, half, 2, share // 2, cols), F32),
            pltpu.VMEM((half, 2, share // 2, cols), F32),
            pltpu.VMEM((half - 1, 2, share // 2, cols), F32),
            pltpu.VMEM((2, half, rows, chunk), F32),
            pltpu.VMEM((half, rows, chunk), F32),
            pltpu.VMEM((half - 1, rows, chunk), F32),
            pltpu.VMEM((n_col, rows, chunk), F32),
            pltpu.VMEM((n_col,) + u_panel.shape, F32),
            pltpu.VMEM((v_below.shape[0], total), BF16),
        ]
        blocks += [pltpu.VMEM((cols, cols), BF16)] * 4
        blocks += [pltpu.VMEM((share, cols), F32)] * 2
        blocks += [pltpu.VMEM((n_col, 2, share // 2, cols), F32)] * 2
        blocks += [pltpu.VMEM((n_col, 2, 2, half, share // 2, cols), F32)] * 2
        blocks += [pltpu.VMEM((rhs, u_panel.shape[1]), F32)]
        counts = [(8,), (2, 2, half), (2, 2, half), (n_row - 1,), (2,), (1,), (1,), (half - 1,), (half - 1,), (1,), (1,), (half - 1,), (half - 1,)]
        counts += [(n_col - 1,)] * 2 + [(3,)] * 2 + [(2, n_col, n_col), (2, n_col)] + [(2, n_col, 2, half - 1)] * 2 + [(2, n_col, 2, half)] * 2 + [(2, n_col)] * 2
        w_rest, x_rest, x_panel = pl.pallas_call(
            functools.partial(chain_kernel, n_row, n_col),
            out_shape=(
                jax.ShapeDtypeStruct(b_rest.shape, F32),
                jax.ShapeDtypeStruct(v_below.shape, F32),
                jax.ShapeDtypeStruct((rows, rhs), F32),
            ),
            in_specs=[anywhere] * 8,
            out_specs=(vm,) * 3,
            scratch_shapes=blocks + [pltpu.SemaphoreType.DMA(shape) for shape in counts],
            compiler_params=pltpu.CompilerParams(vmem_limit_bytes=40 << 20, collective_id=0, has_side_effects=True),
        )(*(pltpu.with_memory_space_constraint(x, pltpu.HBM) for x in (u_diag, l_diag, b_panel, l_below, v_below, u_panel, b_rest, piv)))
        return pl.pallas_call(
            store_kernel,
            out_shape=(
                jax.ShapeDtypeStruct(b_rest.shape, F32),
                jax.ShapeDtypeStruct((rows, rhs), F32),
                jax.ShapeDtypeStruct(v_below.shape, F32),
            ),
            in_specs=[vm] * 3,
            out_specs=(anywhere,) * 3,
            scratch_shapes=[pltpu.SemaphoreType.DMA((3,))],
            compiler_params=pltpu.CompilerParams(vmem_limit_bytes=8 << 20),
        )(w_rest, x_panel, x_rest)
    pack, extra, coup, pick = pl.pallas_call(
        functools.partial(prep_kernel, pre),
        out_shape=(
            jax.ShapeDtypeStruct((rows, cols + chunk), F32),
            jax.ShapeDtypeStruct((rows, cols), F32),
            jax.ShapeDtypeStruct((rhs, cols), F32),
            jax.ShapeDtypeStruct((total, chunk), F32),
        ),
        in_specs=[vm] * 6,
        out_specs=(vm,) * 4,
        compiler_params=params,
    )(u_diag, l_diag, b_panel, l_below, v_below, piv)

    def everywhere(piece):
        return lax.all_gather(piece, ("prow", "pcol"), axis=0).reshape((n_row, n_col) + piece.shape)

    upan = lax.all_gather(u_panel, "pcol", axis=0, tiled=True)
    csum = lax.psum_scatter(coup, "prow", scatter_dimension=0, tiled=True)
    xsum = lax.psum_scatter(pick, "prow", scatter_dimension=0, tiled=True)
    x_panel = lax.all_gather(xsum, "pcol", axis=1, tiled=True)
    w_rest, x_rest = pl.pallas_call(
        functools.partial(main_kernel, pre),
        out_shape=(jax.ShapeDtypeStruct(b_rest.shape, F32), jax.ShapeDtypeStruct(v_below.shape, F32)),
        in_specs=[vm] * 7,
        out_specs=(vm, vm),
        scratch_shapes=halves,
        compiler_params=params,
    )(everywhere(pack), everywhere(extra), everywhere(csum), upan, b_rest, v_below, piv)
    return w_rest, x_panel, x_rest


def solution(mesh):
    in_specs = (
        P("prow", None),
        P("prow", None),
        P("prow", "pcol"),
        P("pcol", "prow"),
        P("prow", "pcol"),
        P("prow", "pcol"),
        P("prow", None),
        P(),
    )
    out_specs = (P("prow", None), P("prow", None), P("prow", None))
    step = functools.partial(body, mesh.shape["prow"], mesh.shape["pcol"])
    return jax.shard_map(step, mesh=mesh, in_specs=in_specs, out_specs=out_specs, check_vma=False)
```

```python
import functools

import jax
import jax.numpy as jnp
from jax import lax
from jax.experimental import pallas as pl
from jax.experimental.pallas import tpu as pltpu
from jax.sharding import PartitionSpec as P

F32 = jnp.float32
BF16 = jnp.bfloat16
NN = (((1,), (0,)), ((), ()))
TN = (((0,), (0,)), ((), ()))
NT = (((1,), (1,)), ((), ()))
BLOCK = 128
MESH = pl.DeviceIdType.MESH


def split(x):
    high = x.astype(BF16)
    return high, (x - high.astype(F32)).astype(BF16)


def dot(left, right, dims):
    return lax.dot_general(left, right, dims, preferred_element_type=F32)


def dot3(left, right, dims=NN):
    (lh, ll), (rh, rl) = left, right
    return dot(lh, rh, dims) + (dot(lh, rl, dims) + dot(ll, rh, dims))


def inverse(square, upper):
    size = square.shape[0]
    row = lax.broadcasted_iota(jnp.int32, (size, size), 0)
    col = lax.broadcasted_iota(jnp.int32, (size, size), 1)
    eye = jnp.where(row == col, 1.0, 0.0)
    if upper:
        on_diag = jnp.where(row == col, square, 0.0)
        strict = jnp.where(col > row, square, 0.0) / jnp.sum(on_diag, axis=1, keepdims=True)
    else:
        strict = jnp.where(col < row, square, 0.0)
    result = eye - strict
    halves = split(strict)
    power = dot3(halves, halves)
    reach = 2
    while reach < size:
        halves = split(power)
        result = result + dot3(split(result), halves)
        reach *= 2
        if reach < size:
            power = dot3(halves, halves)
    if upper:
        result = result / jnp.sum(on_diag, axis=0, keepdims=True)
    return result


def prep_kernel(pre, u_ref, l_ref, b_ref, lb_ref, vb_ref, piv_ref, pack_ref, extra_ref, coup_ref, pick_ref):
    i = lax.axis_index("prow")
    j = lax.axis_index("pcol")
    cols = u_ref.shape[1]
    chunk = pick_ref.shape[1]
    mine = pl.ds(pl.multiple_of(j * chunk, chunk), chunk)
    ratio = cols // u_ref.shape[0]
    pack_ref[:, :cols] = jnp.where(i // ratio > j, l_ref[...], u_ref[...])
    pack_ref[:, cols:] = b_ref[:, mine]
    extra_ref[...] = l_ref[...]
    if pre:

        @pl.when(i // ratio == j)
        def _():
            at = pl.multiple_of((i % ratio) * BLOCK, BLOCK)
            pack_ref[:, pl.ds(at, BLOCK)] = inverse(u_ref[:, pl.ds(at, BLOCK)], True)
            extra_ref[:, pl.ds(at, BLOCK)] = inverse(l_ref[:, pl.ds(at, BLOCK)], False)

    coup_ref[...] = dot3(split(vb_ref[...]), split(lb_ref[...]), TN)
    pick_rows(i, vb_ref, piv_ref, pick_ref, mine)


def pick_rows(i, vb_ref, piv_ref, pick_ref, mine):
    rows = vb_ref.shape[0]
    total = piv_ref.shape[1]
    local = piv_ref[...] - i * rows
    hot = jnp.where(lax.broadcasted_iota(jnp.int32, (rows, total), 0) == local, 1.0, 0.0).astype(BF16)
    part = vb_ref[:, mine]
    first, _ = split(part)
    second = (part - first.astype(F32)).astype(BF16)
    third = (part - first.astype(F32) - second.astype(F32)).astype(BF16)
    pick_ref[...] = dot(hot, first, TN) + dot(hot, second, TN) + dot(hot, third, TN)


def assemble(n_row, n_col, g_ref, e_ref, uh, ul, lh, ll, bs):
    rows, cols = e_ref.shape[2:]
    chunk = g_ref.shape[3] - cols
    for a in range(n_row):
        for b in range(n_col):
            rs = slice(a * rows, (a + 1) * rows)
            cs_ = slice(b * cols, (b + 1) * cols)
            place = a // (cols // rows)
            if place <= b:
                uh[rs, cs_], ul[rs, cs_] = split(g_ref[a, b, :, :cols])
            if place == b:
                lh[rs, cs_], ll[rs, cs_] = split(e_ref[a, b])
            if place > b:
                lh[rs, cs_], ll[rs, cs_] = split(g_ref[a, b, :, :cols])
            bs[rs, b * chunk : (b + 1) * chunk] = g_ref[a, b, :, cols:]


def first_solve(bs, cs, wh, wl, uh, ul, service):
    for p in range(bs.shape[0] // BLOCK):
        first = p * BLOCK
        sl = slice(first, first + BLOCK)
        rhs = bs[sl, :].T
        if p:
            rhs = rhs - dot3((wh[:, :first], wl[:, :first]), (uh[:first, sl], ul[:first, sl]))
        out = dot3(split(rhs), (uh[sl, sl], ul[sl, sl]))
        cs[:, sl] = out
        wh[:, sl], wl[:, sl] = split(out)
        service(p)


def rest_update(wh, wl, columns, br_ref, wr_ref):
    tile = 256
    for t in range(wr_ref.shape[0] // tile):
        ts = slice(t * tile, (t + 1) * tile)
        wr_ref[ts, :] = br_ref[ts, :] - dot3((wh[...], wl[...]), split(columns(ts))).T


def second_solve(cs, wh, wl, lh, ll):
    total = cs.shape[1]
    for p in reversed(range(total // BLOCK)):
        last = (p + 1) * BLOCK
        sl = slice(p * BLOCK, last)
        rhs = cs[:, sl]
        if last < total:
            rhs = rhs - dot3((wh[:, last:], wl[:, last:]), (lh[last:, sl], ll[last:, sl]))
        wh[:, sl], wl[:, sl] = split(dot3(split(rhs), (lh[sl, sl], ll[sl, sl])))


def interchange(i, wh, wl, vb_ref, piv_ref, xr_ref):
    tile = 256
    all_rows, total = vb_ref.shape[0], piv_ref.shape[1]
    for t in range(all_rows // tile):
        ts = slice(t * tile, (t + 1) * tile)
        local = piv_ref[...] - (i * all_rows + t * tile)
        hot = jnp.where(lax.broadcasted_iota(jnp.int32, (tile, total), 0) == local, 1.0, 0.0)
        used = jnp.sum(hot, axis=1, keepdims=True) > 0.5
        hot = hot.astype(BF16)
        new = dot(hot, wh[...], NT) + dot(hot, wl[...], NT)
        xr_ref[ts, :] = jnp.where(used, new, vb_ref[ts, :])


def unpack_diagonal(packed):
    size = packed.shape[0]
    row = lax.broadcasted_iota(jnp.int32, (size, size), 0)
    col = lax.broadcasted_iota(jnp.int32, (size, size), 1)
    upper = jnp.where(col >= row, packed, 0.0)
    lower = jnp.where(col < row, packed, jnp.where(col == row, 1.0, 0.0))
    return upper, lower


def chain_kernel(n, m, u_hbm, l_hbm, b_hbm, lb_hbm, vb_hbm, up_hbm, br_hbm, piv_hbm, wr, xr, xp,
                 piv_ref, part_ref, u_ref, l_ref, b_ref, lb_ref, gm, gh, gl, bt, bp, cp, cy, cz, pk, py, pz, xparts, gu, hot_ref,
                 uih, uil, lih, lil, rb, rv, ww, vv, aw, av, acc,
                 load_s, ring_s, ring_r, b_s, b_r, cy_s, cy_r, cz_s, cz_r, py_s, py_r, pz_s, pz_r, x_s, x_r,
                 up_s, up_r, row_s, row_r, agz_s, agz_r, agy_s, agy_r, sib_s, sib_r):
    i = lax.axis_index("prow")
    j = lax.axis_index("pcol")
    half = n // 2
    rows, cols = u_ref.shape
    share = wr.shape[1] // n
    z, y = i // 2, i % 2
    core = j % 2
    odd = i % 2
    pos = odd * (n - 1 - i // 2) + (1 - odd) * (i // 2)

    def member(at):
        at = (at + n) % n
        back = at // half
        return (1 - back) * 2 * at + back * (2 * (n - 1 - at) + 1)

    right, left = member(pos + 1), member(pos - 1)
    across = (j + m // 2) % m
    beside = j + 1 - 2 * (j % 2)
    over = i + 1 - 2 * (i % 2)

    barrier = pltpu.get_barrier_semaphore()
    for d in range(1, n):
        pl.semaphore_signal(barrier, inc=1, device_id=((i + d) % n, j), device_id_type=MESH)
    for d in range(1, m):
        pl.semaphore_signal(barrier, inc=1, device_id=(i, (j + d) % m), device_id_type=MESH)

    loads = []
    for src, dst in ((u_hbm, u_ref), (l_hbm, l_ref), (b_hbm, b_ref), (lb_hbm, lb_ref), (vb_hbm, xr), (br_hbm, wr), (up_hbm, gu.at[j]), (piv_hbm, piv_ref)):
        loads.append(pltpu.make_async_copy(src, dst, load_s.at[len(loads)]))
        loads[-1].start()

    pending = []

    def guard(cond, action):
        if cond is None:
            action()
        else:
            pl.when(cond)(action)

    def send(src, dst, s_sem, r_sem, to, cond=None):
        copy = pltpu.make_async_remote_copy(src_ref=src, dst_ref=dst, send_sem=s_sem, recv_sem=r_sem, device_id=to, device_id_type=MESH)
        guard(cond, copy.start)
        pending.append((cond, copy))

    def receive(dst, s_sem, r_sem, frm, cond=None):
        copy = pltpu.make_async_remote_copy(src_ref=dst, dst_ref=dst, send_sem=s_sem, recv_sem=r_sem, device_id=frm, device_id_type=MESH)
        guard(cond, copy.wait_recv)

    def reach(way, hop, parity):
        return None if hop < half else parity == way

    def emit(slot, s_sem, r_sem):
        for way, to in ((0, right), (1, left)):
            send(slot(i), slot(i), s_sem.at[way, 0], r_sem.at[way, 0], (to, j))

    def advance(slot, s_sem, r_sem, parity, hop):
        for way, to, frm in ((0, right, left), (1, left, right)):
            row = member(pos - hop) if way == 0 else member(pos + hop)
            receive(slot(row), s_sem.at[way, hop - 1], r_sem.at[way, hop - 1], (frm, j), reach(way, hop, parity))
            if hop < half:
                send(slot(row), slot(row), s_sem.at[way, hop], r_sem.at[way, hop], (to, j), reach(way, hop + 1, parity))

    diagonal = i // 2 == j
    for load in loads[:3]:
        load.wait()
    for h in range(2):
        hs = slice(h * BLOCK, (h + 1) * BLOCK)
        gm[i, h] = jnp.where(i // 2 + (1 - h) * odd > j, l_ref[:, hs], u_ref[:, hs])

    @pl.when(diagonal)
    def _():
        at = pl.multiple_of(odd * BLOCK, BLOCK)
        row = lax.broadcasted_iota(jnp.int32, (BLOCK, BLOCK), 0)
        col = lax.broadcasted_iota(jnp.int32, (BLOCK, BLOCK), 1)
        gm[i, odd] = jnp.where(col >= row, inverse(u_ref[:, pl.ds(at, BLOCK)], True), inverse(l_ref[:, pl.ds(at, BLOCK)], False))
        turned = b_ref[...].T
        for c in range(2):
            for a in range(n):
                first = (c * n + a % 2 * half + a // 2) * share // 2
                bt[a, c] = turned[first : first + share // 2, :]

    pl.semaphore_wait(barrier, n + m - 2)

    def factor(h):
        return lambda row: gm.at[row, h]

    for h in range(2):
        emit(factor(h), ring_s.at[h], ring_r.at[h])
    for d in range(1, n):
        to = (i + d) % n
        send(bt.at[to], bp.at[odd], b_s.at[d - 1], b_r.at[odd], (to, j), diagonal)

    @pl.when(diagonal)
    def _():
        bp[odd] = bt[i]

    loads[6].wait()
    send(gu.at[j], gu.at[j], up_s.at[0], up_r.at[0], (i, across))
    send(gu.at[j], gu.at[j], up_s.at[1], up_r.at[1], (i, beside))

    def fold_start(part, arrive, y_s, y_r):
        send(part.at[1 - y], arrive, y_s, y_r, (over, j))

    def fold_middle(part, arrive, ends, y_s, y_r, z_s, z_r):
        receive(arrive, y_s, y_r, (over, j))
        part[y] = part[y] + arrive[...]
        for d in range(1, half):
            to = (z + d) % half
            send(part.at[y, to], ends.at[d - 1], z_s.at[d - 1], z_r.at[d - 1], (2 * to + y, j))

    def fold_end(part, ends, z_s, z_r):
        total = part[y, z]
        for d in range(1, half):
            receive(ends.at[d - 1], z_s.at[d - 1], z_r.at[d - 1], (2 * ((z + half - d) % half) + y, j))
            total = total + ends[d - 1]
        return total

    loads[3].wait()
    loads[4].wait()
    coup = dot3(split(xr[...]), split(lb_ref[...]), TN)
    for c in range(2):
        for a in range(n):
            first = (c * n + a % 2 * half + a // 2) * share // 2
            cp[a % 2, a // 2, c] = coup[first : first + share // 2, :]
    fold_start(cp, cy, cy_s.at[0], cy_r.at[0])
    for h in range(2):
        advance(factor(h), ring_s.at[h], ring_r.at[h], (j + h) % 2, 1)

    tile = 256
    chunk = xp.shape[1] // m
    part_ref[...] = xr[:, pl.ds(pl.multiple_of(j * chunk, chunk), chunk)]
    total = piv_ref.shape[1]
    loads[7].wait()
    for t in range(xr.shape[0] // tile):
        ts = slice(t * tile, (t + 1) * tile)
        local = piv_ref[...] - (i * xr.shape[0] + t * tile)
        hot = jnp.where(lax.broadcasted_iota(jnp.int32, (tile, total), 0) == local, 1.0, 0.0)
        hot_ref[ts, :] = hot.astype(BF16)
        used = jnp.sum(hot, axis=1, keepdims=True) > 0.5
        xr[ts, :] = jnp.where(used, 0.0, xr[ts, :])
    for h in range(2):
        advance(factor(h), ring_s.at[h], ring_r.at[h], (j + h) % 2, 2)
    for hop in (3, half):
        for h in range(2):
            advance(factor(h), ring_s.at[h], ring_r.at[h], (j + h) % 2, hop)

    for a in range(n):
        for h in range(2):
            at = (slice(a * rows, (a + 1) * rows), slice(h * BLOCK, (h + 1) * BLOCK))
            gh[at], gl[at] = split(gm[a, h])
    a_up, a_low = unpack_diagonal(gm[2 * j, 0])
    d_up, d_low = unpack_diagonal(gm[2 * j + 1, 1])
    one, two = slice(0, BLOCK), slice(BLOCK, 2 * BLOCK)
    uih[...] = jnp.zeros_like(uih)
    uil[...] = jnp.zeros_like(uil)
    lih[...] = jnp.zeros_like(lih)
    lil[...] = jnp.zeros_like(lil)
    uih[one, one], uil[one, one] = split(a_up)
    uih[two, two], uil[two, two] = split(d_up)
    lih[one, one], lil[one, one] = split(a_low)
    lih[two, two], lil[two, two] = split(d_low)
    corner = dot3(split(a_up), split(gm[2 * j, 1]))
    uih[one, two], uil[one, two] = split(-dot3(split(corner), (uih[two, two], uil[two, two])))
    corner = dot3(split(d_low), split(gm[2 * j + 1, 0]))
    lih[two, one], lil[two, one] = split(-dot3(split(corner), (lih[one, one], lil[one, one])))

    for k in range(2):
        owner = 2 * j + k
        receive(bp.at[k], b_s.at[0], b_r.at[k], (owner, j), owner != i)
        for c in range(2):
            rb[c * share // 2 : (c + 1) * share // 2, k * rows : (k + 1) * rows] = bp[k, c]

    def stage(s, forward, out_ref, rhs, inv_h, inv_l):
        lane = 0 if forward else 1

        def later(q):
            return q > s if forward else q < s

        @pl.when(j == s)
        def _():
            if not forward:
                rhs[...] = rhs[...] - fold_end(cp, cz, cz_s, cz_r).reshape(rhs.shape)
            out = dot3(split(rhs[...]), (inv_h[...], inv_l[...]))
            out_ref[s] = out.reshape(out_ref.shape[1:])
            if forward:
                rv[...] = out

        for q in list(range(s + 1, m)) + list(range(s - 1, -1, -1)) if forward else list(range(s - 1, -1, -1)) + list(range(s + 1, m)):
            if later(q):
                send(out_ref.at[s], out_ref.at[s], row_s.at[lane, s, q], row_r.at[lane, s], (i, q), j == s)
                receive(out_ref.at[s], row_s.at[lane, s, q], row_r.at[lane, s], (i, s), j == q)
            else:
                send(out_ref.at[s, q % 2], out_ref.at[s, q % 2], row_s.at[lane, s, q], row_r.at[lane, s], (i, q), j == s)
                receive(out_ref.at[s, q % 2], row_s.at[lane, s, q], row_r.at[lane, s], (i, s), j == q)

        @pl.when(later(j))
        def _():
            rs = slice(s * cols, (s + 1) * cols)
            rhs[...] = rhs[...] - dot3(split(out_ref[s].reshape(rhs.shape)), (gh[rs, :], gl[rs, :]))

    def line(way, k):
        reached = z >= k if way == 0 else z + k < half
        return reached, (z + (half - k if way == 0 else k)) % half

    def spread(lane, s, direct=False):
        whole = (aw, av)[lane]
        own = whole.at[s, core, y, z]
        whole[s, core, y, z] = (ww, vv)[lane][s, core]
        if direct:
            for d in range(1, half):
                send(own, own, agz_s.at[lane, s, 0, d - 1], agz_r.at[lane, s, 0, d - 1], (2 * ((z + d) % half) + y, j))
        else:
            for way in (0, 1):
                there, to = line(1 - way, 1)
                send(own, own, agz_s.at[lane, s, way, 0], agz_r.at[lane, s, way, 0], (2 * to + y, j), there)
        send(own, own, agy_s.at[lane, s, 0, 0], agy_r.at[lane, s, 0, 0], (over, j))

    def onward(lane, s, k):
        for way in (0, 1):
            reached, frm = line(way, k)
            there, to = line(1 - way, 1)
            slot = (aw, av)[lane].at[s, core, y, frm]
            receive(slot, agz_s.at[lane, s, way, k - 1], agz_r.at[lane, s, way, k - 1], (2 * ((z + (half - 1 if way == 0 else 1)) % half) + y, j), reached)
            if k < half - 1:
                send(slot, slot, agz_s.at[lane, s, way, k], agz_r.at[lane, s, way, k], (2 * to + y, j), reached & there)
            send(slot, slot, agy_s.at[lane, s, way, k], agy_r.at[lane, s, way, k], (over, j), reached)

    def onward_direct(lane, s):
        for d in range(1, half):
            frm = (z + half - d) % half
            slot = (aw, av)[lane].at[s, core, y, frm]
            receive(slot, agz_s.at[lane, s, 0, d - 1], agz_r.at[lane, s, 0, d - 1], (2 * frm + y, j))
            send(slot, slot, agy_s.at[lane, s, 0, d], agy_r.at[lane, s, 0, d], (over, j))

    def complete(lane, s, direct=False):
        whole = (aw, av)[lane]
        receive(whole.at[s, core, 1 - y, z], agy_s.at[lane, s, 0, 0], agy_r.at[lane, s, 0, 0], (over, j))
        for d in range(1, half):
            if direct:
                receive(whole.at[s, core, 1 - y, (z + half - d) % half], agy_s.at[lane, s, 0, d], agy_r.at[lane, s, 0, d], (over, j))
            else:
                for way in (0, 1):
                    reached, frm = line(way, d)
                    receive(whole.at[s, core, 1 - y, frm], agy_s.at[lane, s, way, d], agy_r.at[lane, s, way, d], (over, j), reached)
        send(whole.at[s, core], whole.at[s, core], sib_s.at[lane, s], sib_r.at[lane, s], (i, beside))

    def gathered(lane, s):
        whole = (aw, av)[lane]
        receive(whole.at[s, 1 - core], sib_s.at[lane, s], sib_r.at[lane, s], (i, beside))
        halves = split(whole[s].reshape(2 * n * share // 2, cols))
        if lane == 0:
            for t in range(acc.shape[1] // tile):
                ts = slice(t * tile, (t + 1) * tile)
                add = dot3(halves, split(gu[s, :, ts]))
                acc[:, ts] = add if s == 0 else acc[:, ts] + add
        else:
            cs = slice(s * cols, (s + 1) * cols)
            for t in range(xr.shape[0] // tile):
                ts = slice(t * tile, (t + 1) * tile)
                xr[ts, :] += dot(hot_ref[ts, cs], halves[0], NT) + dot(hot_ref[ts, cs], halves[1], NT)

    def fold_x():
        xparts[j] = fold_end(pk, pz, pz_s, pz_r)
        for d in range(1, m):
            send(xparts.at[j], xparts.at[j], x_s.at[d - 1], x_r.at[d - 1], (i, (j + d) % m))

    def near_u():
        receive(gu.at[beside], up_s.at[1], up_r.at[1], (i, beside))

    def cross_u():
        receive(gu.at[across], up_s.at[0], up_r.at[0], (i, across))
        send(gu.at[across], gu.at[across], up_s.at[2], up_r.at[2], (i, beside))

    def far_u():
        far = (across + 1) - 2 * (across % 2)
        receive(gu.at[far], up_s.at[2], up_r.at[2], (i, beside))

    def finish_w():
        loads[5].wait()
        for t in range(wr.shape[0] // tile):
            ts = slice(t * tile, (t + 1) * tile)
            wr[ts, :] = wr[ts, :] - acc[:, ts].T

    def pick():
        part = part_ref[...]
        first, _ = split(part)
        second = (part - first.astype(F32)).astype(BF16)
        third = (part - first.astype(F32) - second.astype(F32)).astype(BF16)
        picked = dot(hot_ref[...], first, TN) + dot(hot_ref[...], second, TN) + dot(hot_ref[...], third, TN)
        for a in range(n):
            pk[a % 2, a // 2] = picked[a * rows : (a + 1) * rows, :]

    W, V = 0, 1
    order = [(W, s) for s in range(m)] + [(V, s) for s in reversed(range(m))]
    last = order[-1]

    def solve(step):
        lane, s = order[step]
        if lane == 0:
            stage(s, True, ww, rb, uih, uil)
        else:
            stage(s, False, vv, rv, lih, lil)
        spread(lane, s, order[step] == last)

    late = len(order) - 1

    def serve(step):
        for k in range(1, half):
            for at in range(late):
                if when(at, k) == step:
                    onward(*order[at], k)
        for at in range(late):
            if when(at, half) == step:
                complete(*order[at])

    def when(at, k):
        step = at
        for _ in range(k):
            step += 2 if step < late and at < m else 1
        return step

    fold_middle(cp, cy, cz, cy_s.at[0], cy_r.at[0], cz_s, cz_r)
    pl.when(j >= m // 2)(pick)
    for step in range(len(order)):
        solve(step)
        serve(step)
        if step == 2:
            pl.when(j < m // 2)(pick)
            fold_start(pk, py, py_s.at[0], py_r.at[0])
        if step == 3:
            near_u()
        if step == 5:
            fold_middle(pk, py, pz, py_s.at[0], py_r.at[0], pz_s, pz_r)
    serve(8)
    cross_u()
    onward_direct(*last)
    serve(9)
    fold_x()
    far_u()
    gathered(W, 0)
    serve(10)
    complete(*last, True)
    gathered(W, 1)
    gathered(V, 3)
    gathered(V, 2)
    gathered(V, 1)
    gathered(W, 2)
    gathered(W, 3)
    gathered(*last)
    finish_w()
    for d in range(1, m):
        frm = (j - d + m) % m
        receive(xparts.at[frm], x_s.at[d - 1], x_r.at[d - 1], (i, frm))
    for q in range(m):
        xp[:, q * chunk : (q + 1) * chunk] = xparts[q]
    for cond, copy in pending:
        guard(cond, copy.wait_send)


def store_kernel(w_ref, p_ref, x_ref, w_out, p_out, x_out, sems):
    copies = [pltpu.make_async_copy(a, b, sems.at[k]) for k, (a, b) in enumerate(((w_ref, w_out), (x_ref, x_out), (p_ref, p_out)))]
    for copy in copies:
        copy.start()
    for copy in copies:
        copy.wait()


def main_kernel(pre, g_ref, e_ref, c_ref, up_ref, br_ref, vb_ref, piv_ref, wr_ref, xr_ref, uh, ul, lh, ll, bs, cs, wh, wl):
    n_row, n_col, crow, cols = c_ref.shape
    assemble(n_row, n_col, g_ref, e_ref, uh, ul, lh, ll, bs)
    if not pre:
        for p in range(uh.shape[0] // BLOCK):
            sl = slice(p * BLOCK, (p + 1) * BLOCK)
            uh[sl, sl], ul[sl, sl] = split(inverse(uh[sl, sl].astype(F32) + ul[sl, sl].astype(F32), True))
            lh[sl, sl], ll[sl, sl] = split(inverse(lh[sl, sl].astype(F32) + ll[sl, sl].astype(F32), False))
    first_solve(bs, cs, wh, wl, uh, ul, lambda p: None)
    for a in range(n_row):
        for b in range(n_col):
            cs[a * crow : (a + 1) * crow, b * cols : (b + 1) * cols] -= c_ref[a, b]
    rest_update(wh, wl, lambda ts: up_ref[:, ts], br_ref, wr_ref)
    second_solve(cs, wh, wl, lh, ll)
    interchange(lax.axis_index("prow"), wh, wl, vb_ref, piv_ref, xr_ref)


def body(n_row, n_col, b_panel, b_rest, u_diag, u_panel, l_diag, l_below, v_below, pivot):
    rows, cols = u_diag.shape
    total, rhs = pivot.shape[0], b_panel.shape[1]
    chunk = rhs // n_col
    pre = rows == BLOCK
    piv = pivot[None, :]
    vm = pl.BlockSpec(memory_space=pltpu.VMEM)
    params = pltpu.CompilerParams(vmem_limit_bytes=56 << 20)
    halves = [pltpu.VMEM((total, total), BF16)] * 4
    halves += [pltpu.VMEM((total, rhs), F32), pltpu.VMEM((rhs, total), F32)]
    halves += [pltpu.VMEM((rhs, total), BF16)] * 2
    if pre and n_row == 8 and n_col == 4:
        half, share = n_row // 2, rhs // n_row
        anywhere = pl.BlockSpec(memory_space=pltpu.HBM)
        blocks = [
            pltpu.VMEM(piv.shape, jnp.int32),
            pltpu.VMEM((v_below.shape[0], chunk), F32),
            pltpu.VMEM((rows, cols), F32),
            pltpu.VMEM((rows, cols), F32),
            pltpu.VMEM((rows, rhs), F32),
            pltpu.VMEM(l_below.shape, F32),
            pltpu.VMEM((n_row, 2, rows, BLOCK), F32),
            pltpu.VMEM((total, cols), BF16),
            pltpu.VMEM((total, cols), BF16),
            pltpu.VMEM((n_row, 2, share // 2, rows), F32),
            pltpu.VMEM((2, 2, share // 2, rows), F32),
            pltpu.VMEM((2, half, 2, share // 2, cols), F32),
            pltpu.VMEM((half, 2, share // 2, cols), F32),
            pltpu.VMEM((half - 1, 2, share // 2, cols), F32),
            pltpu.VMEM((2, half, rows, chunk), F32),
            pltpu.VMEM((half, rows, chunk), F32),
            pltpu.VMEM((half - 1, rows, chunk), F32),
            pltpu.VMEM((n_col, rows, chunk), F32),
            pltpu.VMEM((n_col,) + u_panel.shape, F32),
            pltpu.VMEM((v_below.shape[0], total), BF16),
        ]
        blocks += [pltpu.VMEM((cols, cols), BF16)] * 4
        blocks += [pltpu.VMEM((share, cols), F32)] * 2
        blocks += [pltpu.VMEM((n_col, 2, share // 2, cols), F32)] * 2
        blocks += [pltpu.VMEM((n_col, 2, 2, half, share // 2, cols), F32)] * 2
        blocks += [pltpu.VMEM((rhs, u_panel.shape[1]), F32)]
        counts = [(8,), (2, 2, half), (2, 2, half), (n_row - 1,), (2,), (1,), (1,), (half - 1,), (half - 1,), (1,), (1,), (half - 1,), (half - 1,)]
        counts += [(n_col - 1,)] * 2 + [(3,)] * 2 + [(2, n_col, n_col), (2, n_col)] + [(2, n_col, 2, half - 1)] * 2 + [(2, n_col, 2, half)] * 2 + [(2, n_col)] * 2
        w_rest, x_rest, x_panel = pl.pallas_call(
            functools.partial(chain_kernel, n_row, n_col),
            out_shape=(
                jax.ShapeDtypeStruct(b_rest.shape, F32),
                jax.ShapeDtypeStruct(v_below.shape, F32),
                jax.ShapeDtypeStruct((rows, rhs), F32),
            ),
            in_specs=[anywhere] * 8,
            out_specs=(vm,) * 3,
            scratch_shapes=blocks + [pltpu.SemaphoreType.DMA(shape) for shape in counts],
            compiler_params=pltpu.CompilerParams(vmem_limit_bytes=40 << 20, collective_id=0, has_side_effects=True),
        )(*(pltpu.with_memory_space_constraint(x, pltpu.HBM) for x in (u_diag, l_diag, b_panel, l_below, v_below, u_panel, b_rest, piv)))
        return pl.pallas_call(
            store_kernel,
            out_shape=(
                jax.ShapeDtypeStruct(b_rest.shape, F32),
                jax.ShapeDtypeStruct((rows, rhs), F32),
                jax.ShapeDtypeStruct(v_below.shape, F32),
            ),
            in_specs=[vm] * 3,
            out_specs=(anywhere,) * 3,
            scratch_shapes=[pltpu.SemaphoreType.DMA((3,))],
            compiler_params=pltpu.CompilerParams(vmem_limit_bytes=8 << 20),
        )(w_rest, x_panel, x_rest)
    pack, extra, coup, pick = pl.pallas_call(
        functools.partial(prep_kernel, pre),
        out_shape=(
            jax.ShapeDtypeStruct((rows, cols + chunk), F32),
            jax.ShapeDtypeStruct((rows, cols), F32),
            jax.ShapeDtypeStruct((rhs, cols), F32),
            jax.ShapeDtypeStruct((total, chunk), F32),
        ),
        in_specs=[vm] * 6,
        out_specs=(vm,) * 4,
        compiler_params=params,
    )(u_diag, l_diag, b_panel, l_below, v_below, piv)

    def everywhere(piece):
        return lax.all_gather(piece, ("prow", "pcol"), axis=0).reshape((n_row, n_col) + piece.shape)

    upan = lax.all_gather(u_panel, "pcol", axis=0, tiled=True)
    csum = lax.psum_scatter(coup, "prow", scatter_dimension=0, tiled=True)
    xsum = lax.psum_scatter(pick, "prow", scatter_dimension=0, tiled=True)
    x_panel = lax.all_gather(xsum, "pcol", axis=1, tiled=True)
    w_rest, x_rest = pl.pallas_call(
        functools.partial(main_kernel, pre),
        out_shape=(jax.ShapeDtypeStruct(b_rest.shape, F32), jax.ShapeDtypeStruct(v_below.shape, F32)),
        in_specs=[vm] * 7,
        out_specs=(vm, vm),
        scratch_shapes=halves,
        compiler_params=params,
    )(everywhere(pack), everywhere(extra), everywhere(csum), upan, b_rest, v_below, piv)
    return w_rest, x_panel, x_rest


def solution(mesh):
    in_specs = (
        P("prow", None),
        P("prow", None),
        P("prow", "pcol"),
        P("pcol", "prow"),
        P("prow", "pcol"),
        P("prow", "pcol"),
        P("prow", None),
        P(),
    )
    out_specs = (P("prow", None), P("prow", None), P("prow", None))
    step = functools.partial(body, mesh.shape["prow"], mesh.shape["pcol"])
    return jax.shard_map(step, mesh=mesh, in_specs=in_specs, out_specs=out_specs, check_vma=False)
```
